32 devices in a mesh: mesh: 8 (over y, x, core), band: 4 (over z).
Axes of the slice: x: 2, y: 2, z: 4, core: 2. Of those that a mesh axis runs over, the one named last changes fastest.
Arguments:
- states: float32 [2, 64, 8192], P(None, 'band', 'mesh'), may hold values from -6 to 6
- frozen: float32 [2, 32, 8192], P(None, 'band', 'mesh'), may hold values from -0.125 to 0.125
- weights: float32 [8, 8192], P(None, 'mesh'), may hold values from 0.1 to 1
- potential: float32 [8192], P('mesh'), may hold values from -2 to 2
- send_list: int32 [8, 8, 256], P('mesh'), may hold values from 0 to 1023
- neighbours: int32 [8, 8192], P(None, 'mesh'), may hold values from 0 to 3071, as said below
Outputs:
- evolved: float32 [2, 64, 8192], P(None, 'band', 'mesh')
The draws below stay inside these ranges and needn't reach their ends.
Inputs may be any that keep to these rules, and one draw needn't show every extreme that they name: `neighbours`: an entry below 1024 names a point of the same part; an entry 1024 + s * 256 + c names ghost slot c from part s, where part s is at most 3 parts away in the cyclic order of parts or exactly half the number of parts away, and every part names ghost slots from all those parts. Slots of send_list[s, i] that part i never names hold arbitrary points of part s.
All inputs are finite; a program needn't handle non-finite values.
Results may differ from the reference program's by a relative error of at most 0.0001.
Values sent between devices are 32-bit elements; how exact they have to be, the bound alone decides.
No kernel may reach another device: no remote copies, remote signals or barrier semaphores. Data moves between devices by JAX's collectives and lax.ppermute only.
A program may use at most 128 MiB of HBM per device.

```python
import math
import jax
import jax.numpy as jnp
from jax import lax

PTS_DEV = 1024
CAP = 256
REACH = 3
NBRS = 8
TERMS = 4
NPTS = 8192
NS = 64
NX = 32
N_MESH = 8


def reach_offsets():
    upward = jnp.arange(1, REACH + 1, dtype=jnp.int32)
    return jnp.concatenate([upward, -upward, jnp.array([N_MESH // 2], dtype=jnp.int32)])


def count_table(key):
    parts = N_MESH
    sender = jnp.arange(parts, dtype=jnp.int32)[:, None]
    receiver = jnp.arange(parts, dtype=jnp.int32)[None, :]
    base = jax.random.randint(jax.random.fold_in(key, 1), (parts, parts), CAP // 4, CAP + 1, dtype=jnp.int32)
    relative = (sender - receiver) % parts
    touching = (relative >= 1) & (relative <= REACH) | (relative >= parts - REACH) | (relative == parts // 2)
    choose = jax.random.randint(jax.random.fold_in(key, 2), (parts,), 0, 2 * REACH + 1, dtype=jnp.int32)
    chosen = (receiver - reach_offsets()[choose][None, :]) % parts
    table = jnp.where(sender == chosen, CAP, jnp.where(touching, base, 0)).astype(jnp.int32)
    return table.at[parts - 1, 0].set(CAP)


def draw_neighbours(key, part):
    table = count_table(jax.random.fold_in(key, 5))
    total = N_MESH * PTS_DEV
    owner = (jnp.arange(total, dtype=jnp.int32) // PTS_DEV)[None, :]
    shape = (NBRS, total)
    ghostly = jax.random.randint(jax.random.fold_in(key, 11), shape, 0, 10, dtype=jnp.int32) < 3
    own_pick = jax.random.randint(jax.random.fold_in(key, 12), shape, 0, PTS_DEV, dtype=jnp.int32)
    choose = jax.random.randint(jax.random.fold_in(key, 13), shape, 0, 2 * REACH + 1, dtype=jnp.int32)
    sender = (owner - reach_offsets()[choose]) % N_MESH
    limit = table[sender, jnp.broadcast_to(owner, shape)]
    slot = jax.random.randint(jax.random.fold_in(key, 14), shape, 0, limit, dtype=jnp.int32)
    ghost_index = PTS_DEV + sender * CAP + slot
    result = jnp.where(ghostly, ghost_index, own_pick).astype(jnp.int32)
    result = result.at[0, 0].set(0)
    result = result.at[1, 0].set(PTS_DEV + N_MESH * CAP - 1)
    return result.astype(jnp.int32)


def with_ends(values, rng, smallest, high):
    shape = values.shape
    spot = [jax.random.randint(jax.random.fold_in(rng, axis), (), 0, shape[axis]) for axis in range(len(shape))]
    values = values.at[tuple(spot)].set(smallest)
    longest = shape.index(max(shape))
    spot[longest] = (spot[longest] + 1) % shape[longest]
    return values.at[tuple(spot)].set(high)


def block_levels(rng, shape, shards, least, top_value):
    factor_of, own = 1.0, jax.random.fold_in(rng, 6)
    for axis_at, blocks in shards:
        draws = jnp.exp(jax.random.uniform(jax.random.fold_in(own, axis_at), (blocks,), jnp.float32, least / len(shards), top_value / len(shards)))
        factor_of = factor_of * jnp.repeat(draws, shape[axis_at] // blocks).reshape([-1 if axis == axis_at else 1 for axis in range(len(shape))])
    return factor_of


def scatter_about(stream_key, extent, width, reach, cuts=(), kind=jnp.bfloat16):
    values = width * jax.random.normal(stream_key, extent, jnp.float32)
    if cuts:
        values = values * block_levels(stream_key, extent, cuts, -0.22, 0.18)
    return jnp.clip(values, -reach, reach).astype(kind)


def setup_inputs(seed: int = 0) -> dict:
    key_list = jax.random.split(jax.random.key(seed), 7)
    states = scatter_about(key_list[0], (2, NS, NPTS), 1.0, 6.0, ((1, 4), (2, 8)), jnp.float32)
    frozen = scatter_about(key_list[1], (2, NX, NPTS), (NPTS // 4) ** -0.5, 0.125, ((1, 4), (2, 8)), jnp.float32)
    weights = jnp.clip(jnp.exp(math.log(1.0) - 2.3025851 * jax.random.uniform(key_list[2], (NBRS, NPTS), jnp.float32) ** block_levels(key_list[2], (NBRS, NPTS), ((1, 8),), -0.2, 0.2)), 0.1, 1.0)
    potential = jnp.clip(jax.random.uniform(key_list[3], (NPTS,), jnp.float32, -2.0, 2.0) * block_levels(key_list[3], (NPTS,), ((0, 8),), -0.4, 0.0), -2.0, 2.0)
    send_list = with_ends(jax.random.randint(key_list[4], (N_MESH, N_MESH, CAP), 0, PTS_DEV), jax.random.fold_in(key_list[4], 1), 0, PTS_DEV - 1).astype(jnp.int32)
    neighbours = draw_neighbours(jax.random.fold_in(key_list[6], 71), 0)
    return {"states": states, "frozen": frozen, "weights": weights, "potential": potential, "send_list": send_list, "neighbours": neighbours}


time_step = 0.3


def rotate(field):
    return jnp.stack([field[1], -field[0]])


def reference(states, frozen, weights, potential, send_list, neighbours):
    parts = N_MESH
    points = PTS_DEV
    starts = jnp.arange(parts, dtype=jnp.int32)[:, None, None] * points
    sources = jnp.transpose(starts + send_list, (1, 0, 2)).reshape(parts, parts * CAP)
    owner = jnp.arange(parts * points, dtype=jnp.int32) // points
    ghost_slot = jnp.maximum(neighbours - points, 0).astype(jnp.int32)
    global_index = jnp.where(neighbours < points, owner[None, :] * points + neighbours, sources[owner[None, :], ghost_slot]).astype(jnp.int32)

    def apply_hamiltonian(field):
        stencil = jnp.zeros_like(field)
        for order in range(NBRS):
            stencil = stencil + weights[order] * (field[:, :, global_index[order]] - field)
        paired = jnp.stack([field, rotate(field)])
        intersection = jnp.einsum("cmp,ocjp->omj", frozen, paired, precision=lax.Precision.HIGHEST)
        blocks = jnp.stack([jnp.stack([intersection[0], -intersection[1]]), jnp.stack([intersection[1], intersection[0]])])
        exchange = jnp.einsum("dmp,cdmj->cjp", frozen, blocks, precision=lax.Precision.HIGHEST)
        return -0.5 * stencil + potential * field - exchange

    total = states
    term = states
    for order in range(1, TERMS + 1):
        image = apply_hamiltonian(term)
        term = (time_step / order) * rotate(image)
        total = total + term
    return total
```

```python
import functools

import jax
import jax.numpy as jnp
from jax import lax
from jax.experimental import pallas as pl
from jax.experimental.pallas import tpu as pltpu
from jax.sharding import PartitionSpec as P

TERMS = 4
REACH = 3
LANES = 128
TILE = 256

time_step = 0.3

F32, BF16 = jnp.float32, jnp.bfloat16
VMEM_LIMIT = 48 << 20


def split(value):
    high = value.astype(BF16)
    return high, (value - high.astype(F32)).astype(BF16)


def stacked(value):
    high, low = split(value)
    return jnp.concatenate([high, low], axis=0), high


def matmul(left, right):
    return lax.dot_general(left, right, (((1,), (0,)), ((), ())), preferred_element_type=F32)


def matmul_transposed(left, right):
    return lax.dot_general(left, right, (((1,), (1,)), ((), ())), preferred_element_type=F32)


def blocks_of(parts):
    if parts == 8:
        return list(range(8))
    relative = [0]
    for offset in [*range(1, REACH + 1), *range(-REACH, 0), parts // 2]:
        if offset % parts not in relative:
            relative.append(offset % parts)
    return relative


def receiver_of(me, block, parts):
    return me ^ block if parts == 8 else lax.rem(me + block, parts)


def block_of(sender, me, parts):
    if parts == 8:
        return sender ^ me
    relative = lax.rem(me - sender + parts, parts)
    result = jnp.zeros_like(relative)
    for place, block in enumerate(blocks_of(parts)):
        result = jnp.where(relative == block, place, result)
    return result


def call(kernel, out_shape, cost, *args, scalars=0):
    spaces = [pl.BlockSpec(memory_space=pltpu.SMEM if at < scalars else pltpu.VMEM) for at in range(len(args))]
    outs = [pl.BlockSpec(memory_space=pltpu.VMEM)] * len(out_shape)
    return pl.pallas_call(
        kernel,
        out_shape=[jax.ShapeDtypeStruct(shape, dtype) for shape, dtype in out_shape],
        in_specs=spaces,
        out_specs=outs,
        compiler_params=pltpu.CompilerParams(vmem_limit_bytes=VMEM_LIMIT),
        cost_estimate=pl.CostEstimate(flops=cost[0], bytes_accessed=cost[1], transcendentals=0),
    )(*args)


def pack_kernel(parts, me_ref, states_ref, routes_ref, select_ref, payload_ref):
    points = states_ref.shape[1]
    capacity = routes_ref.shape[1]
    rows = states_ref.shape[0]
    both, _ = stacked(states_ref[...])
    me = me_ref[0]
    row_id = lax.broadcasted_iota(jnp.int32, (points, capacity), 0)
    for place, block in enumerate(blocks_of(parts)):
        route = routes_ref[pl.ds(receiver_of(me, block, parts), 1), :]
        one_hot = jnp.where(row_id == route, 1.0, 0.0).astype(BF16)
        select_ref[:, pl.ds(place * capacity, capacity)] = one_hot
        if place:
            packed = matmul(both, one_hot)
            payload_ref[place - 1] = packed[:rows] + packed[rows:]


def stencil_kernel(parts, capacity, me_ref, neighbours_ref, weights_ref, potential_ref, near_high, near_low, far_high, far_low, diagonal_ref):
    count, points = neighbours_ref.shape
    me = me_ref[0]
    named = neighbours_ref[...]
    ghost = jnp.maximum(named - points, 0)
    sender = ghost // capacity
    place = block_of(sender, me, parts)
    named = jnp.where(named < points, named, points + place * capacity + (ghost - sender * capacity))
    half = 0.5 * weights_ref[...]
    diagonal_ref[...] = jnp.sum(half, axis=0, keepdims=True) + potential_ref[...]
    targets = [named[k : k + 1] for k in range(count)]
    values = [half[k : k + 1] for k in range(count)]
    for k in range(count):
        for later in range(k + 1, count):
            same = targets[k] == targets[later]
            values[k] = jnp.where(same, values[k] + values[later], values[k])
            targets[later] = jnp.where(same, -1, targets[later])
    tall = 16
    near_tiles = near_high.shape[0] // TILE
    tiles = near_tiles + far_high.shape[0] // TILE
    row_id = lax.broadcasted_iota(jnp.int32, (tall, LANES), 0).astype(F32).astype(BF16)
    zero = jnp.zeros((tall, LANES), BF16)
    for lane in range(0, points, LANES):
        at = [jnp.broadcast_to(t[:, lane : lane + LANES], (tall, LANES)) for t in targets]
        pieces = [split(jnp.broadcast_to(v[:, lane : lane + LANES], (tall, LANES))) for v in values]

        def tile_rows(high_ref, low_ref, first, tile):
            local = [
                jnp.where(a // TILE == tile, a - tile * TILE, -1).astype(F32).astype(BF16)
                for a in at
            ]
            for row in range(0, TILE, tall):
                here = row_id + jnp.asarray(row, BF16)
                high, low = zero, zero
                for k in range(count):
                    hit = local[k] == here
                    high = jnp.where(hit, pieces[k][0], high)
                    low = jnp.where(hit, pieces[k][1], low)
                start = pl.multiple_of((tile - first) * TILE + row, tall)
                high_ref[pl.ds(start, tall), lane : lane + LANES] = high
                low_ref[pl.ds(start, tall), lane : lane + LANES] = low

        @pl.loop(0, near_tiles)
        def _(tile):
            tile_rows(near_high, near_low, 0, tile)

        @pl.loop(near_tiles, tiles)
        def _(tile):
            tile_rows(far_high, far_low, near_tiles, tile)


def frozen_kernel(frozen_ref, states_ref, wide_high, wide_low, partial_ref):
    groups, _, vectors, points = frozen_ref.shape
    real = jnp.concatenate([frozen_ref[g, 0] for g in range(groups)], axis=0)
    imag = jnp.concatenate([frozen_ref[g, 1] for g in range(groups)], axis=0)
    wide = jnp.concatenate(
        [jnp.concatenate([real, imag], axis=1), jnp.concatenate([-imag, real], axis=1)], axis=0
    )
    high, low = split(wide)
    wide_high[...] = high
    wide_low[...] = low
    partial_ref[...] = intersect(states_ref[...], high, low)


def intersect(term, wide_high, wide_low):
    half = term.shape[0] // 2
    line = jnp.concatenate([term[:half], term[half:]], axis=1)
    both, high = stacked(line)
    result = matmul_transposed(both, wide_high)
    result = result[:half] + result[half:] + matmul_transposed(high, wide_low)
    columns = result.shape[1]
    if columns >= LANES:
        return result
    fold = LANES // columns
    tall = half // fold
    return jnp.concatenate([result[i * tall : (i + 1) * tall] for i in range(fold)], axis=1)


def unfold(folded, half, columns):
    if columns >= LANES:
        return folded
    fold = LANES // columns
    return jnp.concatenate([folded[:, i * columns : (i + 1) * columns] for i in range(fold)], axis=0)


def apply_exchange(total, half, wide_high, wide_low):
    both, high = stacked(unfold(total, half, wide_high.shape[0]))
    result = matmul(both, wide_high)
    result = result[:half] + result[half:] + matmul(high, wide_low)
    points = result.shape[1] // 2
    return jnp.concatenate([result[:, :points], result[:, points:]], axis=0)


def near_kernel(term_ref, select_ref, near_high, near_low, diagonal_ref, base_ref):
    rows, points = term_ref.shape
    term = term_ref[...]
    both, high = stacked(term)
    own = matmul(both, select_ref[:, : near_high.shape[0] - points])
    own_both, own_high = stacked(own[:rows] + own[rows:])
    value = matmul(both, near_high[:points]) + matmul(own_both, near_high[points:])
    low = matmul(high, near_low[:points]) + matmul(own_high, near_low[points:])
    base_ref[...] = term * diagonal_ref[...] - (value[:rows] + value[rows:] + low)


def far_kernel(order, last, first, *refs):
    if first:
        ghosts_ref, sums_ref, base_ref, total_ref, select_ref, far_high, far_low, wide_high, wide_low = refs[:9]
        outs = refs[9:]
    else:
        ghosts_ref, sums_ref, base_ref, total_ref, select_ref, far_high, far_low, wide_high, wide_low = refs[:9]
        outs = refs[9:]
    rows = base_ref.shape[0]
    half = rows // 2
    blocks = ghosts_ref.shape[0]
    capacity = ghosts_ref.shape[2]
    if first:
        sums = sums_ref[...]
    else:
        width = sums_ref.shape[1]
        sums = sums_ref[...]
        for block in range(blocks):
            sums = sums + ghosts_ref[block, rows:, :width]
    image = base_ref[...] - apply_exchange(sums, half, wide_high[...], wide_low[...])
    pieces = [stacked(ghosts_ref[block, :rows, :]) for block in range(blocks)]
    both = jnp.concatenate([piece[0] for piece in pieces], axis=1)
    high = jnp.concatenate([piece[1] for piece in pieces], axis=1)
    far = matmul(both, far_high[...])
    image = image - (far[:rows] + far[rows:] + matmul(high, far_low[...]))
    scale = time_step / order
    term = jnp.concatenate([scale * image[half:], -scale * image[:half]], axis=0)
    outs[0][...] = total_ref[...] + term
    if last:
        return
    _, term_ref, payload_ref, partial_ref = outs
    term_ref[...] = term
    both, _ = stacked(term)
    partial = intersect(term, wide_high[...], wide_low[...])
    partial_ref[...] = partial
    tall, width = partial.shape
    if width < capacity:
        partial = jnp.concatenate([partial, jnp.zeros((tall, capacity - width), F32)], axis=1)
    for block in range(blocks):
        packed = matmul(both, select_ref[:, pl.ds((block + 1) * capacity, capacity)])
        payload_ref[block, :rows, :] = packed[:rows] + packed[rows:]
        payload_ref[block, rows:, :] = partial


def swap(value, bits, parts):
    return lax.ppermute(value, "mesh", [(part, part ^ bits) for part in range(parts)])


def exchange(payload, parts):
    if parts == 8:
        across = [
            swap(payload[2 * chip - 1 : 2 * chip + 1], 2 * chip, parts) for chip in range(1, 4)
        ]
        passed = jnp.concatenate([payload[:1]] + [block[1:] for block in across], axis=0)
        passed = swap(passed, 1, parts)
        order = [passed[:1]]
        for chip in range(3):
            order += [across[chip][:1], passed[chip + 1 : chip + 2]]
        return jnp.concatenate(order, axis=0)
    arrived = [
        lax.ppermute(payload[at], "mesh", [(part, (part + block) % parts) for part in range(parts)])
        for at, block in enumerate(blocks_of(parts)[1:])
    ]
    return jnp.stack(arrived)


def add_up(partial, parts):
    if parts == 8:
        pair = partial + swap(partial, 1, parts)
        return pair + swap(pair, 2, parts) + swap(pair, 4, parts) + swap(pair, 6, parts)
    return lax.psum(partial, "mesh")


def gather_frozen(frozen):
    bands = lax.axis_size("band")
    if bands <= 4:
        pieces = [frozen]
        for step in range(1, bands):
            pieces.append(lax.ppermute(frozen, "band", [(at, (at + step) % bands) for at in range(bands)]))
        return jnp.stack(pieces)
    return lax.all_gather(frozen, "band", axis=0, tiled=False)


def body(states, frozen, weights, potential, send_list, neighbours):
    parts = lax.axis_size("mesh")
    points = states.shape[2]
    rows = 2 * states.shape[1]
    capacity = send_list.shape[2]
    places = len(blocks_of(parts))
    me = lax.axis_index("mesh").astype(jnp.int32).reshape(1)
    field = states.reshape(rows, points)
    routes = send_list[0]

    select, payload = call(
        functools.partial(pack_kernel, parts),
        [((points, places * capacity), BF16), ((places - 1, rows, capacity), F32)],
        (4 * rows * points * places * capacity, 4 << 20),
        me, field, routes, scalars=1,
    )
    ghosts = exchange(payload, parts)
    full_frozen = gather_frozen(frozen)
    near_rows, far_rows = points + capacity, (places - 1) * capacity
    near_high, near_low, far_high, far_low, diagonal = call(
        functools.partial(stencil_kernel, parts, capacity),
        [((near_rows, points), BF16)] * 2 + [((far_rows, points), BF16)] * 2 + [((1, points), F32)],
        (6 * (near_rows + far_rows) * points, 12 << 20),
        me, neighbours, weights, potential.reshape(1, points), scalars=1,
    )
    vectors = full_frozen.shape[0] * full_frozen.shape[2]
    columns = 2 * vectors
    half = rows // 2
    sum_shape = (half, columns) if columns >= LANES else (half * columns // LANES, LANES)
    wide_high, wide_low, partial = call(
        frozen_kernel,
        [((columns, 2 * points), BF16)] * 2 + [(sum_shape, F32)],
        (6 * columns * points * rows, 2 << 20),
        full_frozen, field,
    )
    sums = add_up(partial, parts)
    total, term = field, field
    for order in range(1, TERMS + 1):
        (base,) = call(
            near_kernel,
            [((rows, points), F32)],
            (6 * rows * points * near_rows, 8 << 20),
            term, select, near_high, near_low, diagonal,
        )
        last = order == TERMS
        shapes = [((rows, points), F32)]
        if not last:
            shapes += [
                ((rows, points), F32),
                ((places - 1, rows + sum_shape[0], capacity), F32),
                (sum_shape, F32),
            ]
        outs = call(
            functools.partial(far_kernel, order, last, order == 1),
            shapes,
            (6 * rows * points * far_rows, 12 << 20),
            ghosts, sums, base, total, select, far_high, far_low, wide_high, wide_low,
        )
        total = outs[0]
        if not last:
            _, term, payload, sums = outs
            ghosts = exchange(payload, parts)
    return total.reshape(states.shape)


def solution(mesh):
    return jax.shard_map(
        body,
        mesh=mesh,
        in_specs=(
            P(None, "band", "mesh"),
            P(None, "band", "mesh"),
            P(None, "mesh"),
            P("mesh"),
            P("mesh", None, None),
            P(None, "mesh"),
        ),
        out_specs=P(None, "band", "mesh"),
        check_vma=False,
    )
```

```python
import functools

import jax
import jax.numpy as jnp
from jax import lax
from jax.experimental import pallas as pl
from jax.experimental.pallas import tpu as pltpu
from jax.sharding import PartitionSpec as P

TERMS = 4
REACH = 3
LANES = 128
TILE = 256

time_step = 0.3

F32, BF16 = jnp.float32, jnp.bfloat16
VMEM_LIMIT = 24 << 20


def split(value):
    high = value.astype(BF16)
    return high, (value - high.astype(F32)).astype(BF16)


def stacked(value):
    high, low = split(value)
    return jnp.concatenate([high, low], axis=0), high


def dot(left, right):
    return lax.dot_general(left, right, (((1,), (0,)), ((), ())), preferred_element_type=F32)


def product(both, high, right_high, right_low):
    rows = high.shape[0]
    result = dot(both, right_high)
    return result[:rows] + result[rows:] + dot(high, right_low)


def blocks_of(parts):
    if parts == 8:
        return [0, 2, 4, 6, 1, 3, 5, 7]
    relative = [0]
    for offset in [*range(1, REACH + 1), *range(-REACH, 0), parts // 2]:
        if offset % parts not in relative:
            relative.append(offset % parts)
    return relative


EARLY = 3


def receiver_of(me, block, parts):
    return me ^ block if parts == 8 else lax.rem(me + block, parts)


def place_of(sender, me, parts):
    relative = sender ^ me if parts == 8 else lax.rem(me - sender + parts, parts)
    result = jnp.zeros_like(relative)
    for place, block in enumerate(blocks_of(parts)):
        result = jnp.where(relative == block, place, result)
    return result


def call(kernel, out_shape, cost, *args, scalars=0):
    spaces = [pl.BlockSpec(memory_space=pltpu.SMEM if at < scalars else pltpu.VMEM) for at in range(len(args))]
    outs = [pl.BlockSpec(memory_space=pltpu.VMEM)] * len(out_shape)
    return pl.pallas_call(
        kernel,
        out_shape=[jax.ShapeDtypeStruct(shape, dtype) for shape, dtype in out_shape],
        in_specs=spaces,
        out_specs=outs,
        compiler_params=pltpu.CompilerParams(vmem_limit_bytes=VMEM_LIMIT),
        cost_estimate=pl.CostEstimate(flops=cost[0], bytes_accessed=cost[1], transcendentals=0),
    )(*args)


def stencil_rows(targets, values, outs, first):
    tall = 16
    points = targets[0].shape[1]
    row_id = lax.broadcasted_iota(jnp.int32, (tall, LANES), 0).astype(jnp.int16)
    zero = jnp.zeros((tall, LANES), BF16)
    for lane in range(0, points, LANES):
        at = [jnp.broadcast_to(t[:, lane : lane + LANES], (tall, LANES)) for t in targets]
        pieces = [split(jnp.broadcast_to(v[:, lane : lane + LANES], (tall, LANES))) for v in values]
        base = first
        for high_ref, low_ref in outs:

            @pl.loop(0, high_ref.shape[0] // TILE)
            def _(tile, base=base, high_ref=high_ref, low_ref=low_ref):
                local = [(a - (base + tile * TILE)).astype(jnp.int16) for a in at]
                for row in range(0, TILE, tall):
                    here = row_id + jnp.int16(row)
                    high, low = zero, zero
                    for target, (value_high, value_low) in zip(local, pieces, strict=True):
                        hit = target == here
                        high = jnp.where(hit, value_high, high)
                        low = jnp.where(hit, value_low, low)
                    start = pl.multiple_of(tile * TILE + row, tall)
                    high_ref[pl.ds(start, tall), lane : lane + LANES] = high
                    low_ref[pl.ds(start, tall), lane : lane + LANES] = low

            base = base + high_ref.shape[0]


def plan_kernel(parts, capacity, me_ref, neighbours_ref, weights_ref, potential_ref, routes_ref, targets_ref, values_ref, diagonal_ref, select_ref, near_high, near_low):
    count, points = neighbours_ref.shape
    me = me_ref[0]
    named = neighbours_ref[...]
    ghost = jnp.maximum(named - points, 0)
    sender = ghost // capacity
    place = place_of(sender, me, parts)
    named = jnp.where(named < points, named, points + place * capacity + (ghost - sender * capacity))
    half = 0.5 * weights_ref[...]
    diagonal_ref[...] = jnp.sum(half, axis=0, keepdims=True) + potential_ref[...]
    targets = [named[k : k + 1] for k in range(count)]
    values = [half[k : k + 1] for k in range(count)]
    for k in range(count):
        for later in range(k + 1, count):
            same = targets[k] == targets[later]
            values[k] = jnp.where(same, values[k] + values[later], values[k])
            targets[later] = jnp.where(same, -1, targets[later])
    for k in range(count):
        targets_ref[k : k + 1] = targets[k]
        values_ref[k : k + 1] = values[k]
    row_id = lax.broadcasted_iota(jnp.int32, (points, capacity), 0)
    for place, block in enumerate(blocks_of(parts)):
        route = routes_ref[pl.ds(receiver_of(me, block, parts), 1), :]
        select_ref[:, pl.ds(place * capacity, capacity)] = jnp.where(row_id == route, 1.0, 0.0).astype(BF16)
    stencil_rows(targets, values, [(near_high, near_low)], 0)


def ghost_kernel(first, targets_ref, values_ref, *outs):
    count = targets_ref.shape[0]
    targets = [targets_ref[k : k + 1] for k in range(count)]
    values = [values_ref[k : k + 1] for k in range(count)]
    stencil_rows(targets, values, list(zip(outs[::2], outs[1::2], strict=True)), first)


def intersect(both, high, turned_high, turned_low):
    half = high.shape[0] // 2
    columns = turned_high.shape[1] // 2
    result = product(both, high, turned_high, turned_low)
    if columns >= LANES:
        return result[:half, :columns] + result[half:, columns:]
    result = result[:half] + pltpu.roll(result[half:], columns, 1)
    lane = lax.broadcasted_iota(jnp.int32, (half // 2, LANES), 1)
    return jnp.where(lane < columns, result[: half // 2], pltpu.roll(result[half // 2 :], columns, 1))


def exchange_term(sums, half, wide_high, wide_low):
    columns = wide_high.shape[0] // 2
    if columns >= LANES:
        zero = jnp.zeros_like(sums)
        left = jnp.concatenate([jnp.concatenate([sums, zero], axis=1), jnp.concatenate([zero, sums], axis=1)], axis=0)
    else:
        lower = lax.broadcasted_iota(jnp.int32, sums.shape, 1) < columns
        rolled = pltpu.roll(sums, columns, 1)
        left = jnp.concatenate(
            [
                jnp.where(lower, sums, 0.0),
                jnp.where(lower, rolled, 0.0),
                jnp.where(lower, 0.0, rolled),
                jnp.where(lower, 0.0, sums),
            ],
            axis=0,
        )
    both, high = stacked(left)
    return product(both, high, wide_high, wide_low)


def send(term, select_ref, turned_high, turned_low, early_refs, late_ref, partial_ref, paired):
    rows = term.shape[0]
    both, high = stacked(term)
    partial = intersect(both, high, turned_high, turned_low)
    partial_ref[...] = partial
    tall, width = partial.shape
    capacity = late_ref.shape[2]
    if width < capacity:
        partial = jnp.concatenate([partial, jnp.zeros((tall, capacity - width), F32)], axis=1)
    late = late_ref.shape[0]
    places = [(ref, 0) for ref in early_refs]
    if paired:
        places += [(late_ref, 0)] + [(ref, 1) for ref in early_refs]
    else:
        places += [(late_ref, at) for at in range(late)]
    for place, (ref, at) in enumerate(places):
        packed = dot(both, select_ref[:, pl.ds((place + 1) * capacity, capacity)])
        ref[at, :rows, :] = packed[:rows] + packed[rows:]
        ref[at, rows:, :] = partial


def start_kernel(paired, frozen_ref, field_ref, select_ref, wide_high, wide_low, turned_high, turned_low, partial_ref, late_ref, *early_refs):
    groups = frozen_ref.shape[0]
    real = jnp.concatenate([frozen_ref[g, 0] for g in range(groups)], axis=0)
    imag = jnp.concatenate([frozen_ref[g, 1] for g in range(groups)], axis=0)
    wide = jnp.concatenate([real, -imag, imag, real], axis=0)
    wide_high[...], wide_low[...] = split(wide)
    high, low = split(wide.T)
    turned_high[...] = high
    turned_low[...] = low
    send(field_ref[...], select_ref, high, low, early_refs, late_ref, partial_ref, paired)


def near_kernel(term_ref, select_ref, near_high, near_low, diagonal_ref, base_ref):
    rows, points = term_ref.shape
    term = term_ref[...]
    both, high = stacked(term)
    own = dot(both, select_ref[:, : near_high.shape[0] - points])
    own_both, own_high = stacked(own[:rows] + own[rows:])
    value = product(both, high, near_high[:points], near_low[:points])
    value = value + product(own_both, own_high, near_high[points:], near_low[points:])
    base_ref[...] = term * diagonal_ref[...] - value


def ghost_values(blocks, high, low):
    pieces = [stacked(block) for block in blocks]
    both = jnp.concatenate([piece[0] for piece in pieces], axis=1)
    return product(both, jnp.concatenate([piece[1] for piece in pieces], axis=1), high, low)


def early_kernel(base_ref, partial_ref, early_high, early_low, *refs):
    early_refs, (base_out, sums_out) = refs[:-2], refs[-2:]
    rows = base_ref.shape[0]
    sums = partial_ref[...]
    for ref in early_refs:
        sums = sums + ref[0, rows:, : sums.shape[1]]
    sums_out[...] = sums
    base_out[...] = base_ref[...] - ghost_values([ref[0, :rows, :] for ref in early_refs], early_high[...], early_low[...])


def late_kernel(order, last, paired, late_ref, base_ref, sums_ref, total_ref, select_ref, late_high, late_low, wide_high, wide_low, turned_high, turned_low, *outs):
    rows = base_ref.shape[0]
    half = rows // 2
    blocks = late_ref.shape[0]
    sums = sums_ref[...]
    for block in range(blocks):
        sums = sums + late_ref[block, rows:, : sums.shape[1]]
    image = base_ref[...] - exchange_term(sums, half, wide_high[...], wide_low[...])
    image = image - ghost_values([late_ref[block, :rows, :] for block in range(blocks)], late_high[...], late_low[...])
    scale = time_step / order
    term = jnp.concatenate([scale * image[half:], -scale * image[:half]], axis=0)
    outs[0][...] = total_ref[...] + term
    if last:
        return
    _, term_ref, partial_ref, late_out, *early_outs = outs
    term_ref[...] = term
    send(term, select_ref, turned_high[...], turned_low[...], early_outs, late_out, partial_ref, paired)


def swap(value, bits, parts):
    return lax.ppermute(value, "mesh", [(part, part ^ bits) for part in range(parts)])


def move(value, offset, parts):
    return lax.ppermute(value, "mesh", [(part, (part + offset) % parts) for part in range(parts)])


def gather_frozen(frozen):
    bands = lax.axis_size("band")
    if bands <= 4:
        pieces = [frozen]
        for step in range(1, bands):
            pieces.append(lax.ppermute(frozen, "band", [(at, (at + step) % bands) for at in range(bands)]))
        return jnp.stack(pieces)
    return lax.all_gather(frozen, "band", axis=0, tiled=False)


def body(states, frozen, weights, potential, send_list, neighbours):
    parts = lax.axis_size("mesh")
    points = states.shape[2]
    rows = 2 * states.shape[1]
    half = rows // 2
    capacity = send_list.shape[2]
    relations = blocks_of(parts)
    places = len(relations)
    paired = parts == 8
    me = lax.axis_index("mesh").astype(jnp.int32).reshape(1)
    field = states.reshape(rows, points)
    count = neighbours.shape[0]

    full_frozen = gather_frozen(frozen)
    near_rows, early_rows, late_rows = points + capacity, EARLY * capacity, (places - 1 - EARLY) * capacity
    targets, values, diagonal, select, near_high, near_low = call(
        functools.partial(plan_kernel, parts, capacity),
        [((count, points), jnp.int32), ((count, points), F32), ((1, points), F32), ((points, places * capacity), BF16)]
        + [((near_rows, points), BF16)] * 2,
        (6 * near_rows * points, 12 << 20),
        me, neighbours, weights, potential.reshape(1, points), send_list[0], scalars=1,
    )
    vectors = full_frozen.shape[0] * full_frozen.shape[2]
    columns = 2 * vectors
    sum_shape = (half, columns) if columns >= LANES else (half * columns // LANES, LANES)
    tall = rows + sum_shape[0]
    outgoing = [(sum_shape, F32), ((1 if paired else places - 1 - EARLY, tall, capacity), F32)]
    outgoing += [((2 if paired else 1, tall, capacity), F32)] * EARLY
    wide_high, wide_low, turned_high, turned_low, partial, late, *early = call(
        functools.partial(start_kernel, paired),
        [((2 * columns, points), BF16)] * 2 + [((points, 2 * columns), BF16)] * 2 + outgoing,
        (6 * rows * points * places * capacity, 4 << 20),
        full_frozen, field, select,
    )
    total, term = field, field
    ghost_matrices = None
    for order in range(1, TERMS + 1):
        if paired:
            early = [swap(block, bits, parts) for block, bits in zip(early, relations[1 : 1 + EARLY], strict=True)]
        else:
            early = [move(block, offset, parts) for block, offset in zip(early, relations[1:], strict=False)]
        if ghost_matrices is None:
            ghost_matrices = call(
                functools.partial(ghost_kernel, near_rows),
                [((early_rows, points), BF16)] * 2 + [((late_rows, points), BF16)] * 2,
                (6 * (early_rows + late_rows) * points, 24 << 20),
                targets, values,
            )
            early_high, early_low, late_high, late_low = ghost_matrices
        (base,) = call(
            near_kernel,
            [((rows, points), F32)],
            (6 * rows * points * near_rows, 16 << 20),
            term, select, near_high, near_low, diagonal,
        )
        if paired:
            late = jnp.concatenate([late] + [block[1:] for block in early], axis=0)
            late, base = lax.optimization_barrier((late, base))
            late = swap(late, 1, parts)
        else:
            late = jnp.stack(
                [move(late[at], offset, parts) for at, offset in enumerate(relations[1 + EARLY :])]
            )
        base, sums = call(
            early_kernel,
            [((rows, points), F32), (sum_shape, F32)],
            (6 * rows * points * early_rows, 4 << 20),
            base, partial, early_high, early_low, *early,
        )
        last = order == TERMS
        shapes = [((rows, points), F32)]
        if not last:
            shapes += [((rows, points), F32)] + outgoing
        outs = call(
            functools.partial(late_kernel, order, last, paired),
            shapes,
            (6 * rows * points * late_rows, 12 << 20),
            late, base, sums, total, select, late_high, late_low, wide_high, wide_low, turned_high, turned_low,
        )
        total = outs[0]
        if not last:
            _, term, partial, late, *early = outs
    return total.reshape(states.shape)


def solution(mesh):
    return jax.shard_map(
        body,
        mesh=mesh,
        in_specs=(
            P(None, "band", "mesh"),
            P(None, "band", "mesh"),
            P(None, "mesh"),
            P("mesh"),
            P("mesh", None, None),
            P(None, "mesh"),
        ),
        out_specs=P(None, "band", "mesh"),
        check_vma=False,
    )
```

```python
import functools

import jax
import jax.numpy as jnp
from jax import lax
from jax.experimental import pallas as pl
from jax.experimental.pallas import tpu as pltpu
from jax.sharding import PartitionSpec as P

TERMS = 4
REACH = 3
LANES = 128
TILE = 256

time_step = 0.3

F32, BF16 = jnp.float32, jnp.bfloat16
VMEM_LIMIT = 24 << 20


def split(value):
    high = value.astype(BF16)
    return high, (value - high.astype(F32)).astype(BF16)


def stacked(value):
    high, low = split(value)
    return jnp.concatenate([high, low], axis=0), high


def dot(left, right):
    return lax.dot_general(left, right, (((1,), (0,)), ((), ())), preferred_element_type=F32)


def product(both, high, right_high, right_low):
    rows = high.shape[0]
    result = dot(both, right_high)
    return result[:rows] + result[rows:] + dot(high, right_low)


def blocks_of(parts):
    if parts == 8:
        return [0, 6, 2, 4, 1, 7, 3, 5]
    relative = [0]
    for offset in [*range(1, REACH + 1), *range(-REACH, 0), parts // 2]:
        if offset % parts not in relative:
            relative.append(offset % parts)
    return relative


EARLY = 3
NEAR_FIRST = 3


def receiver_of(me, block, parts):
    return me ^ block if parts == 8 else lax.rem(me + block, parts)


def place_of(sender, me, parts):
    relative = sender ^ me if parts == 8 else lax.rem(me - sender + parts, parts)
    result = jnp.zeros_like(relative)
    for place, block in enumerate(blocks_of(parts)):
        result = jnp.where(relative == block, place, result)
    return result


def call(kernel, out_shape, cost, *args, scalars=0, remote=0, scratch=()):
    held = slice(scalars, scalars + remote)
    args = list(args)
    args[held] = [pltpu.with_memory_space_constraint(arg, pltpu.HBM) for arg in args[held]]
    spaces = [pltpu.SMEM] * scalars + [pltpu.HBM] * remote + [pltpu.VMEM] * (len(args) - scalars - remote)
    return pl.pallas_call(
        kernel,
        out_shape=[jax.ShapeDtypeStruct(shape, dtype) for shape, dtype in out_shape],
        in_specs=[pl.BlockSpec(memory_space=space) for space in spaces],
        out_specs=[pl.BlockSpec(memory_space=pltpu.VMEM)] * len(out_shape),
        scratch_shapes=scratch,
        compiler_params=pltpu.CompilerParams(vmem_limit_bytes=VMEM_LIMIT),
        cost_estimate=pl.CostEstimate(flops=cost[0], bytes_accessed=cost[1], transcendentals=0),
    )(*args)


def stencil_rows(targets, values, outs, first):
    tall = 16
    points = targets[0].shape[1]
    row_id = lax.broadcasted_iota(jnp.int32, (tall, LANES), 0).astype(jnp.int16)
    zero = jnp.zeros((tall, LANES), BF16)
    for lane in range(0, points, LANES):
        at = [jnp.broadcast_to(t[:, lane : lane + LANES], (tall, LANES)) for t in targets]
        pieces = [split(jnp.broadcast_to(v[:, lane : lane + LANES], (tall, LANES))) for v in values]
        base = first
        for high_ref, low_ref in outs:

            @pl.loop(0, high_ref.shape[0] // TILE)
            def _(tile, base=base, high_ref=high_ref, low_ref=low_ref):
                local = [(a - (base + tile * TILE)).astype(jnp.int16) for a in at]
                for row in range(0, TILE, tall):
                    here = row_id + jnp.int16(row)
                    high, low = zero, zero
                    for target, (value_high, value_low) in zip(local, pieces, strict=True):
                        hit = target == here
                        high = jnp.where(hit, value_high, high)
                        low = jnp.where(hit, value_low, low)
                    start = pl.multiple_of(tile * TILE + row, tall)
                    high_ref[pl.ds(start, tall), lane : lane + LANES] = high
                    low_ref[pl.ds(start, tall), lane : lane + LANES] = low

            base = base + high_ref.shape[0]


def plan_kernel(parts, paired, me_ref, *refs):
    sources, refs = refs[:6], refs[6:]
    targets_ref, values_ref, diagonal_ref, select_ref, near_high, near_low, field_ref, frozen_ref, late_ref, *refs = refs
    early_refs, (routes_ref, neighbours_ref, weights_ref, potential_ref, arrival) = refs[:-5], refs[-5:]
    arrays = [routes_ref, field_ref, neighbours_ref, weights_ref, potential_ref, frozen_ref]
    copies = [
        pltpu.make_async_copy(source, array, arrival.at[at])
        for at, (source, array) in enumerate(zip(sources, arrays, strict=True))
    ]
    for copy in copies:
        copy.start()
    count, points = neighbours_ref.shape
    capacity = routes_ref.shape[2]
    rows = field_ref.shape[0]
    me = me_ref[0]
    copies[0].wait()
    copies[1].wait()
    row_id = lax.broadcasted_iota(jnp.int32, (points, capacity), 0)
    for place, block in enumerate(blocks_of(parts)):
        route = routes_ref[0, pl.ds(receiver_of(me, block, parts), 1), :]
        select_ref[:, pl.ds(place * capacity, capacity)] = jnp.where(row_id == route, 1.0, 0.0).astype(BF16)
    both, _ = stacked(field_ref[...])
    pack(both, select_ref, early_refs, late_ref, paired)
    for copy in copies[2:]:
        copy.wait()
    named = neighbours_ref[...]
    ghost = jnp.maximum(named - points, 0)
    sender = ghost // capacity
    place = place_of(sender, me, parts)
    named = jnp.where(named < points, named, points + place * capacity + (ghost - sender * capacity))
    half = 0.5 * weights_ref[...]
    diagonal_ref[...] = jnp.sum(half, axis=0, keepdims=True) + potential_ref[...]
    targets = [named[k : k + 1] for k in range(count)]
    values = [half[k : k + 1] for k in range(count)]
    for k in range(count):
        for later in range(k + 1, count):
            same = targets[k] == targets[later]
            values[k] = jnp.where(same, values[k] + values[later], values[k])
            targets[later] = jnp.where(same, -1, targets[later])
    for k in range(count):
        targets_ref[k : k + 1] = targets[k]
        values_ref[k : k + 1] = values[k]
    stencil_rows(targets, values, [(near_high, near_low)], 0)


def ghost_kernel(first, targets_ref, values_ref, *outs):
    count = targets_ref.shape[0]
    targets = [targets_ref[k : k + 1] for k in range(count)]
    values = [values_ref[k : k + 1] for k in range(count)]
    stencil_rows(targets, values, list(zip(outs[::2], outs[1::2], strict=True)), first)


def intersect(both, high, turned_high, turned_low):
    half = high.shape[0] // 2
    columns = turned_high.shape[1] // 2
    result = product(both, high, turned_high, turned_low)
    if columns >= LANES:
        return result[:half, :columns] + result[half:, columns:]
    result = result[:half] + pltpu.roll(result[half:], columns, 1)
    lane = lax.broadcasted_iota(jnp.int32, (half // 2, LANES), 1)
    return jnp.where(lane < columns, result[: half // 2], pltpu.roll(result[half // 2 :], columns, 1))


def exchange_term(sums, half, wide_high, wide_low):
    columns = wide_high.shape[0] // 2
    if columns >= LANES:
        zero = jnp.zeros_like(sums)
        left = jnp.concatenate([jnp.concatenate([sums, zero], axis=1), jnp.concatenate([zero, sums], axis=1)], axis=0)
    else:
        lower = lax.broadcasted_iota(jnp.int32, sums.shape, 1) < columns
        rolled = pltpu.roll(sums, columns, 1)
        left = jnp.concatenate(
            [
                jnp.where(lower, sums, 0.0),
                jnp.where(lower, rolled, 0.0),
                jnp.where(lower, 0.0, rolled),
                jnp.where(lower, 0.0, sums),
            ],
            axis=0,
        )
    both, high = stacked(left)
    return product(both, high, wide_high, wide_low)


def slots_of(early_refs, late_ref, paired):
    slots = [(ref, 0) for ref in early_refs]
    if paired:
        return slots + [(late_ref, 0)] + [(ref, 1) for ref in early_refs]
    return slots + [(late_ref, at) for at in range(late_ref.shape[0])]


def pack(both, select_ref, early_refs, late_ref, paired):
    rows = both.shape[0] // 2
    capacity = late_ref.shape[2]
    for place, (ref, at) in enumerate(slots_of(early_refs, late_ref, paired)):
        packed = dot(both, select_ref[:, pl.ds((place + 1) * capacity, capacity)])
        ref[at, :rows, :] = packed[:rows] + packed[rows:]


def spread(partial, early_refs, late_ref, paired):
    tall, width = partial.shape
    capacity = late_ref.shape[2]
    if width < capacity:
        partial = jnp.concatenate([partial, jnp.zeros((tall, capacity - width), F32)], axis=1)
    for ref, at in slots_of(early_refs, late_ref, paired):
        ref[at, -tall:, :] = partial


def start_kernel(paired, groups, *refs):
    pieces, (field_ref, late_in, *refs) = refs[:groups], refs[groups:]
    early_in, (wide_high, wide_low, turned_high, turned_low, partial_ref, late_ref, *early_refs) = refs[:EARLY], refs[EARLY:]
    rows = field_ref.shape[0]
    pieces = [piece[...] for piece in pieces]
    if pieces[0].ndim == 4:
        pieces = [pieces[0][band] for band in range(pieces[0].shape[0])]
    real = jnp.concatenate([piece[0] for piece in pieces], axis=0)
    imag = jnp.concatenate([piece[1] for piece in pieces], axis=0)
    wide = jnp.concatenate([real, -imag, imag, real], axis=0)
    wide_high[...], wide_low[...] = split(wide)
    turned_high[...], turned_low[...] = split(wide.T)
    both, high = stacked(field_ref[...])
    partial = intersect(both, high, turned_high[...], turned_low[...])
    partial_ref[...] = partial
    for source, target in zip([late_in, *early_in], [late_ref, *early_refs], strict=True):
        target[:, :rows, :] = source[:, :rows, :]
    spread(partial, early_refs, late_ref, paired)


def near_kernel(term_ref, select_ref, first_high, first_low, rest_high, rest_low, diagonal_ref, base_ref):
    rows, points = term_ref.shape
    term = term_ref[...]
    both, high = stacked(term)
    own = dot(both, select_ref[:, : first_high.shape[0] + rest_high.shape[0] - points])
    own_both, own_high = stacked(own[:rows] + own[rows:])
    cut = first_high.shape[0]
    value = product(both[:, :cut], high[:, :cut], first_high[...], first_low[...])
    both = jnp.concatenate([both[:, cut:], own_both], axis=1)
    high = jnp.concatenate([high[:, cut:], own_high], axis=1)
    value = value + product(both, high, rest_high[...], rest_low[...])
    base_ref[...] = term * diagonal_ref[...] - value


def ghost_values(blocks, high, low):
    pieces = [stacked(block) for block in blocks]
    both = jnp.concatenate([piece[0] for piece in pieces], axis=1)
    return product(both, jnp.concatenate([piece[1] for piece in pieces], axis=1), high, low)


def early_kernel(base_ref, partial_ref, early_high, early_low, *refs):
    early_refs, (base_out, sums_out) = refs[:-2], refs[-2:]
    rows = base_ref.shape[0]
    sums = partial_ref[...]
    for ref in early_refs:
        sums = sums + ref[0, rows:, : sums.shape[1]]
    sums_out[...] = sums
    base_out[...] = base_ref[...] - ghost_values([ref[0, :rows, :] for ref in early_refs], early_high[...], early_low[...])


def late_kernel(order, last, paired, late_ref, base_ref, sums_ref, total_ref, select_ref, late_high, late_low, wide_high, wide_low, turned_high, turned_low, *outs):
    rows = base_ref.shape[0]
    half = rows // 2
    blocks = late_ref.shape[0]
    sums = sums_ref[...]
    for block in range(blocks):
        sums = sums + late_ref[block, rows:, : sums.shape[1]]
    image = base_ref[...] - exchange_term(sums, half, wide_high[...], wide_low[...])
    image = image - ghost_values([late_ref[block, :rows, :] for block in range(blocks)], late_high[...], late_low[...])
    scale = time_step / order
    term = jnp.concatenate([scale * image[half:], -scale * image[:half]], axis=0)
    outs[0][...] = total_ref[...] + term
    if last:
        return
    _, term_ref, partial_ref, late_out, *early_outs = outs
    term_ref[...] = term
    both, high = stacked(term)
    partial = intersect(both, high, turned_high[...], turned_low[...])
    partial_ref[...] = partial
    pack(both, select_ref, early_outs, late_out, paired)
    spread(partial, early_outs, late_out, paired)


def swap(value, bits, parts):
    return lax.ppermute(value, "mesh", [(part, part ^ bits) for part in range(parts)])


def move(value, offset, parts):
    return lax.ppermute(value, "mesh", [(part, (part + offset) % parts) for part in range(parts)])


def gather_frozen(frozen):
    bands = lax.axis_size("band")
    if bands <= 4:
        return [lax.ppermute(frozen, "band", [(at, (at + step) % bands) for at in range(bands)]) for step in range(1, bands)]
    return [lax.all_gather(frozen, "band", axis=0, tiled=False)]


def body(states, frozen, weights, potential, send_list, neighbours):
    parts = lax.axis_size("mesh")
    points = states.shape[2]
    rows = 2 * states.shape[1]
    half = rows // 2
    capacity = send_list.shape[2]
    relations = blocks_of(parts)
    places = len(relations)
    paired = parts == 8
    me = lax.axis_index("mesh").astype(jnp.int32).reshape(1)
    count = neighbours.shape[0]

    bands = lax.axis_size("band")
    pieces = gather_frozen(frozen)
    columns = 2 * bands * frozen.shape[1]
    sum_shape = (half, columns) if columns >= LANES else (half * columns // LANES, LANES)
    tall = rows + sum_shape[0]
    outgoing = [((1 if paired else places - 1 - EARLY, tall, capacity), F32)]
    outgoing += [((2 if paired else 1, tall, capacity), F32)] * EARLY
    first_rows = NEAR_FIRST * TILE
    rest_rows = points + capacity - first_rows
    early_rows, late_rows = EARLY * capacity, (places - 1 - EARLY) * capacity
    targets, values, diagonal, select, first_high, first_low, field, own_frozen, late, *early = call(
        functools.partial(plan_kernel, parts, paired),
        [((count, points), jnp.int32), ((count, points), F32), ((1, points), F32), ((points, places * capacity), BF16)]
        + [((first_rows, points), BF16)] * 2
        + [((rows, points), F32), (frozen.shape, F32)]
        + outgoing,
        (6 * first_rows * points, 12 << 20),
        me, send_list, states.reshape(rows, points), neighbours, weights, potential.reshape(1, points), frozen,
        scalars=1,
        remote=6,
        scratch=[
            pltpu.VMEM(send_list.shape, jnp.int32),
            pltpu.VMEM(neighbours.shape, jnp.int32),
            pltpu.VMEM(weights.shape, F32),
            pltpu.VMEM((1, points), F32),
            pltpu.SemaphoreType.DMA((6,)),
        ],
    )
    if len(pieces) == bands - 1:
        pieces = [own_frozen, *pieces]
    wide_high, wide_low, turned_high, turned_low, partial, late, *early = call(
        functools.partial(start_kernel, paired, len(pieces)),
        [((2 * columns, points), BF16)] * 2 + [((points, 2 * columns), BF16)] * 2 + [(sum_shape, F32)] + outgoing,
        (6 * rows * points * 2 * columns, 4 << 20),
        *pieces, field, late, *early,
    )
    total, term = field, field
    for order in range(1, TERMS + 1):
        if paired:
            early = [swap(block, bits, parts) for block, bits in zip(early, relations[1 : 1 + EARLY], strict=True)]
        else:
            early = [move(block, offset, parts) for block, offset in zip(early, relations[1:], strict=False)]
        if order == 1:
            rest_high, rest_low, early_high, early_low = call(
                functools.partial(ghost_kernel, first_rows),
                [((rest_rows, points), BF16)] * 2 + [((early_rows, points), BF16)] * 2,
                (6 * (rest_rows + early_rows) * points, 12 << 20),
                targets, values,
            )
        (base,) = call(
            near_kernel,
            [((rows, points), F32)],
            (6 * rows * points * (first_rows + rest_rows), 16 << 20),
            term, select, first_high, first_low, rest_high, rest_low, diagonal,
        )
        if paired:
            late = jnp.concatenate([late] + [block[1:] for block in early], axis=0)
            late, base, targets = lax.optimization_barrier((late, base, targets))
            late = swap(late, 1, parts)
        else:
            late = jnp.stack(
                [move(late[at], offset, parts) for at, offset in enumerate(relations[1 + EARLY :])]
            )
        if order == 1:
            late_high, late_low = call(
                functools.partial(ghost_kernel, first_rows + rest_rows + early_rows),
                [((late_rows, points), BF16)] * 2,
                (6 * late_rows * points, 12 << 20),
                targets, values,
            )
        base, sums = call(
            early_kernel,
            [((rows, points), F32), (sum_shape, F32)],
            (6 * rows * points * early_rows, 4 << 20),
            base, partial, early_high, early_low, *early,
        )
        last = order == TERMS
        shapes = [((rows, points), F32)]
        if not last:
            shapes += [((rows, points), F32), (sum_shape, F32)] + outgoing
        outs = call(
            functools.partial(late_kernel, order, last, paired),
            shapes,
            (6 * rows * points * late_rows, 12 << 20),
            late, base, sums, total, select, late_high, late_low, wide_high, wide_low, turned_high, turned_low,
        )
        total = outs[0]
        if not last:
            _, term, partial, late, *early = outs
    return total.reshape(states.shape)


def solution(mesh):
    return jax.shard_map(
        body,
        mesh=mesh,
        in_specs=(
            P(None, "band", "mesh"),
            P(None, "band", "mesh"),
            P(None, "mesh"),
            P("mesh"),
            P("mesh", None, None),
            P(None, "mesh"),
        ),
        out_specs=P(None, "band", "mesh"),
        check_vma=False,
    )
```

```python
import functools

import jax
import jax.numpy as jnp
from jax import lax
from jax.experimental import pallas as pl
from jax.experimental.pallas import tpu as pltpu
from jax.sharding import PartitionSpec as P

TERMS = 4
REACH = 3
LANES = 128
TILE = 256

time_step = 0.3

F32, BF16 = jnp.float32, jnp.bfloat16
VMEM_LIMIT = 24 << 20


def split(value):
    high = value.astype(BF16)
    return high, (value - high.astype(F32)).astype(BF16)


def stacked(value):
    high, low = split(value)
    return jnp.concatenate([high, low], axis=0), high


def dot(left, right):
    return lax.dot_general(left, right, (((1,), (0,)), ((), ())), preferred_element_type=F32)


def product(both, high, right_high, right_low):
    rows = high.shape[0]
    result = dot(both, right_high)
    return result[:rows] + result[rows:] + dot(high, right_low)


def blocks_of(parts):
    if parts == 8:
        return [0, 6, 2, 4, 1, 7, 3, 5]
    relative = [0]
    for offset in [*range(1, REACH + 1), *range(-REACH, 0), parts // 2]:
        if offset % parts not in relative:
            relative.append(offset % parts)
    return relative


EARLY = 3
LATE_FIRST = 2


def receiver_of(me, block, parts):
    return me ^ block if parts == 8 else lax.rem(me + block, parts)


def place_of(sender, me, parts):
    relative = sender ^ me if parts == 8 else lax.rem(me - sender + parts, parts)
    result = jnp.zeros_like(relative)
    for place, block in enumerate(blocks_of(parts)):
        result = jnp.where(relative == block, place, result)
    return result


def call(kernel, out_shape, cost, *args, scalars=0, remote=0, scratch=()):
    held = slice(scalars, scalars + remote)
    args = list(args)
    args[held] = [pltpu.with_memory_space_constraint(arg, pltpu.HBM) for arg in args[held]]
    spaces = [pltpu.SMEM] * scalars + [pltpu.HBM] * remote + [pltpu.VMEM] * (len(args) - scalars - remote)
    return pl.pallas_call(
        kernel,
        out_shape=[jax.ShapeDtypeStruct(shape, dtype) for shape, dtype in out_shape],
        in_specs=[pl.BlockSpec(memory_space=space) for space in spaces],
        out_specs=[pl.BlockSpec(memory_space=pltpu.VMEM)] * len(out_shape),
        scratch_shapes=scratch,
        compiler_params=pltpu.CompilerParams(vmem_limit_bytes=VMEM_LIMIT),
        cost_estimate=pl.CostEstimate(flops=cost[0], bytes_accessed=cost[1], transcendentals=0),
    )(*args)


def stencil_rows(targets, values, outs, first):
    tall = 16
    points = targets[0].shape[1]
    row_id = lax.broadcasted_iota(jnp.int32, (tall, LANES), 0).astype(jnp.int16)
    zero = jnp.zeros((tall, LANES), BF16)
    for lane in range(0, points, LANES):
        at = [jnp.broadcast_to(t[:, lane : lane + LANES], (tall, LANES)) for t in targets]
        pieces = [split(jnp.broadcast_to(v[:, lane : lane + LANES], (tall, LANES))) for v in values]
        base = first
        for high_ref, low_ref in outs:

            @pl.loop(0, high_ref.shape[0] // TILE)
            def _(tile, base=base, high_ref=high_ref, low_ref=low_ref):
                local = [(a - (base + tile * TILE)).astype(jnp.int16) for a in at]
                for row in range(0, TILE, tall):
                    here = row_id + jnp.int16(row)
                    high, low = zero, zero
                    for target, (value_high, value_low) in zip(local, pieces, strict=True):
                        hit = target == here
                        high = jnp.where(hit, value_high, high)
                        low = jnp.where(hit, value_low, low)
                    start = pl.multiple_of(tile * TILE + row, tall)
                    high_ref[pl.ds(start, tall), lane : lane + LANES] = high
                    low_ref[pl.ds(start, tall), lane : lane + LANES] = low

            base = base + high_ref.shape[0]


def plan_kernel(parts, me_ref, *refs):
    sources, refs = refs[:6], refs[6:]
    targets_ref, values_ref, diagonal_ref, select_ref, near_high, near_low, field_ref, frozen_ref, *refs = refs
    out, (routes_ref, neighbours_ref, weights_ref, potential_ref, arrival) = refs[:-5], refs[-5:]
    arrays = [routes_ref, field_ref, neighbours_ref, weights_ref, potential_ref, frozen_ref]
    copies = [
        pltpu.make_async_copy(source, array, arrival.at[at])
        for at, (source, array) in enumerate(zip(sources, arrays, strict=True))
    ]
    for copy in copies:
        copy.start()
    count, points = neighbours_ref.shape
    capacity = routes_ref.shape[2]
    rows = field_ref.shape[0]
    me = me_ref[0]
    copies[0].wait()
    copies[1].wait()
    tall = 16
    row_id = lax.broadcasted_iota(jnp.int32, (tall, capacity), 0).astype(jnp.int16)
    one, zero = jnp.ones((tall, capacity), BF16), jnp.zeros((tall, capacity), BF16)
    for place, block in enumerate(blocks_of(parts)):
        route = routes_ref[0, pl.ds(receiver_of(me, block, parts), 1), :]
        route = jnp.broadcast_to(route, (tall, capacity)).astype(jnp.int16)
        for row in range(0, points, tall):
            hit = route == row_id + jnp.int16(row)
            select_ref[row : row + tall, pl.ds(place * capacity, capacity)] = jnp.where(hit, one, zero)
    both, _ = stacked(field_ref[...])
    pack(both, select_ref, out[:-1], out[-1])
    for copy in copies[2:]:
        copy.wait()
    named = neighbours_ref[...]
    ghost = jnp.maximum(named - points, 0)
    sender = ghost // capacity
    place = place_of(sender, me, parts)
    named = jnp.where(named < points, named, points + place * capacity + (ghost - sender * capacity))
    half = 0.5 * weights_ref[...]
    diagonal_ref[...] = jnp.sum(half, axis=0, keepdims=True) + potential_ref[...]
    targets = [named[k : k + 1] for k in range(count)]
    values = [half[k : k + 1] for k in range(count)]
    for k in range(count):
        for later in range(k + 1, count):
            same = targets[k] == targets[later]
            values[k] = jnp.where(same, values[k] + values[later], values[k])
            targets[later] = jnp.where(same, -1, targets[later])
    for k in range(count):
        targets_ref[k : k + 1] = targets[k]
        values_ref[k : k + 1] = values[k]
    stencil_rows(targets, values, [(near_high, near_low)], 0)


def ghost_kernel(first, targets_ref, values_ref, *outs):
    count = targets_ref.shape[0]
    targets = [targets_ref[k : k + 1] for k in range(count)]
    values = [values_ref[k : k + 1] for k in range(count)]
    stencil_rows(targets, values, list(zip(outs[::2], outs[1::2], strict=True)), first)


def intersect(both, high, turned_high, turned_low):
    half = high.shape[0] // 2
    columns = turned_high.shape[1] // 2
    result = product(both, high, turned_high, turned_low)
    if columns >= LANES:
        return result[:half, :columns] + result[half:, columns:]
    result = result[:half] + pltpu.roll(result[half:], columns, 1)
    lane = lax.broadcasted_iota(jnp.int32, (half // 2, LANES), 1)
    return jnp.where(lane < columns, result[: half // 2], pltpu.roll(result[half // 2 :], columns, 1))


def exchange_term(sums, half, wide_high, wide_low):
    columns = wide_high.shape[0] // 2
    if columns >= LANES:
        zero = jnp.zeros_like(sums)
        left = jnp.concatenate([jnp.concatenate([sums, zero], axis=1), jnp.concatenate([zero, sums], axis=1)], axis=0)
    else:
        lower = lax.broadcasted_iota(jnp.int32, sums.shape, 1) < columns
        rolled = pltpu.roll(sums, columns, 1)
        left = jnp.concatenate(
            [
                jnp.where(lower, sums, 0.0),
                jnp.where(lower, rolled, 0.0),
                jnp.where(lower, 0.0, rolled),
                jnp.where(lower, 0.0, sums),
            ],
            axis=0,
        )
    both, high = stacked(left)
    return product(both, high, wide_high, wide_low)


def slots_of(rows, tall, early_refs, late_ref):
    slots = [(ref, 0) for ref in early_refs]
    slots += [(late_ref.at[at], tall) for at in range(late_ref.shape[0])]
    if early_refs[0].shape[0] > rows + tall:
        slots += [(ref, rows + tall) for ref in early_refs]
    return slots


def pack(both, select_ref, early_refs, late_ref):
    rows = both.shape[0] // 2
    capacity = early_refs[0].shape[1]
    tall = late_ref.shape[1] - rows
    for place, (ref, start) in enumerate(slots_of(rows, tall, early_refs, late_ref)):
        packed = dot(both, select_ref[:, pl.ds((place + 1) * capacity, capacity)])
        ref[start : start + rows, :] = packed[:rows] + packed[rows:]


def spread(partial, rows, early_refs, late_ref):
    tall, width = partial.shape
    capacity = early_refs[0].shape[1]
    if width < capacity:
        partial = jnp.concatenate([partial, jnp.zeros((tall, capacity - width), F32)], axis=1)
    for ref in early_refs:
        ref[rows : rows + tall, :] = partial
    for at in range(late_ref.shape[0]):
        late_ref[at, :tall, :] = partial


def start_kernel(groups, *refs):
    pieces, (field_ref, *refs) = refs[:groups], refs[groups:]
    ready, (wide_high, wide_low, turned_high, turned_low, partial_ref, *out) = refs[: EARLY + 1], refs[EARLY + 1 :]
    rows = field_ref.shape[0]
    pieces = [piece[...] for piece in pieces]
    if pieces[0].ndim == 4:
        pieces = [pieces[0][band] for band in range(pieces[0].shape[0])]
    real = jnp.concatenate([piece[0] for piece in pieces], axis=0)
    imag = jnp.concatenate([piece[1] for piece in pieces], axis=0)
    wide = jnp.concatenate([real, -imag, imag, real], axis=0)
    wide_high[...], wide_low[...] = split(wide)
    turned_high[...], turned_low[...] = split(wide.T)
    both, high = stacked(field_ref[...])
    partial = intersect(both, high, turned_high[...], turned_low[...])
    partial_ref[...] = partial
    tall = partial.shape[0]
    (*early_in, late_in), (*early_refs, late_ref) = ready, out
    slots_in = slots_of(rows, tall, early_in, late_in)
    for (source, start), (target, _) in zip(slots_in, slots_of(rows, tall, early_refs, late_ref), strict=True):
        target[start : start + rows, :] = source[start : start + rows, :]
    spread(partial, rows, early_refs, late_ref)


def near_kernel(first, term_ref, select_ref, near_high, near_low, diagonal_ref, *refs):
    if first is not None:
        targets_ref, values_ref, base_ref, *outs = refs
        ghost_kernel(first, targets_ref, values_ref, *outs)
    else:
        (base_ref,) = refs
    rows, points = term_ref.shape
    term = term_ref[...]
    both, high = stacked(term)
    own = dot(both, select_ref[:, : near_high.shape[0] - points])
    own_both, own_high = stacked(own[:rows] + own[rows:])
    both = jnp.concatenate([both, own_both], axis=1)
    high = jnp.concatenate([high, own_high], axis=1)
    base_ref[...] = term * diagonal_ref[...] - product(both, high, near_high[...], near_low[...])


def ghost_values(blocks, high, low):
    pieces = [stacked(block) for block in blocks]
    both = jnp.concatenate([piece[0] for piece in pieces], axis=1)
    return product(both, jnp.concatenate([piece[1] for piece in pieces], axis=1), high, low)


def early_kernel(base_ref, partial_ref, early_high, early_low, *refs):
    early_refs, (base_out, sums_out) = refs[:-2], refs[-2:]
    rows = base_ref.shape[0]
    sums = partial_ref[...]
    tall, width = sums.shape
    for ref in early_refs:
        sums = sums + ref[rows : rows + tall, :width]
    sums_out[...] = sums
    base_out[...] = base_ref[...] - ghost_values([ref[:rows, :] for ref in early_refs], early_high[...], early_low[...])


def late_kernel(order, last, late_ref, base_ref, sums_ref, total_ref, select_ref, first_high, first_low, rest_high, rest_low, wide_high, wide_low, turned_high, turned_low, *outs):
    half = base_ref.shape[0] // 2
    blocks = range(late_ref.shape[0])
    sums = sums_ref[...]
    tall, width = sums.shape
    for block in blocks:
        sums = sums + late_ref[block, :tall, :width]
    ghosts = [late_ref[block, tall:, :] for block in blocks]
    cut = first_high.shape[0] // late_ref.shape[2]
    image = base_ref[...] - exchange_term(sums, half, wide_high[...], wide_low[...])
    image = image - ghost_values(ghosts[:cut], first_high[...], first_low[...])
    image = image - ghost_values(ghosts[cut:], rest_high[...], rest_low[...])
    scale = time_step / order
    term = jnp.concatenate([scale * image[half:], -scale * image[:half]], axis=0)
    outs[0][...] = total_ref[...] + term
    if last:
        return
    _, term_ref, partial_ref, *out = outs
    term_ref[...] = term
    both, high = stacked(term)
    partial = intersect(both, high, turned_high[...], turned_low[...])
    partial_ref[...] = partial
    pack(both, select_ref, out[:-1], out[-1])
    spread(partial, term.shape[0], out[:-1], out[-1])


def swap(value, bits, parts):
    return lax.ppermute(value, "mesh", [(part, part ^ bits) for part in range(parts)])


def move(value, offset, parts):
    return lax.ppermute(value, "mesh", [(part, (part + offset) % parts) for part in range(parts)])


def gather_frozen(frozen):
    bands = lax.axis_size("band")
    if bands <= 4:
        return [lax.ppermute(frozen, "band", [(at, (at + step) % bands) for at in range(bands)]) for step in range(1, bands)]
    return [lax.all_gather(frozen, "band", axis=0, tiled=False)]


def body(states, frozen, weights, potential, send_list, neighbours):
    parts = lax.axis_size("mesh")
    points = states.shape[2]
    rows = 2 * states.shape[1]
    half = rows // 2
    capacity = send_list.shape[2]
    relations = blocks_of(parts)
    places = len(relations)
    paired = parts == 8
    me = lax.axis_index("mesh").astype(jnp.int32).reshape(1)
    count = neighbours.shape[0]

    bands = lax.axis_size("band")
    pieces = gather_frozen(frozen)
    columns = 2 * bands * frozen.shape[1]
    sum_shape = (half, columns) if columns >= LANES else (half * columns // LANES, LANES)
    tall = rows + sum_shape[0]
    late_blocks = places - 1 - EARLY
    outgoing = [((tall + rows if paired else tall, capacity), F32)] * EARLY
    outgoing += [((late_blocks - EARLY if paired else late_blocks, tall, capacity), F32)]
    near_rows, early_rows = points + capacity, EARLY * capacity
    first_rows = LATE_FIRST * capacity
    rest_rows = late_blocks * capacity - first_rows
    targets, values, diagonal, select, near_high, near_low, field, own_frozen, *sent = call(
        functools.partial(plan_kernel, parts),
        [((count, points), jnp.int32), ((count, points), F32), ((1, points), F32), ((points, places * capacity), BF16)]
        + [((near_rows, points), BF16)] * 2
        + [((rows, points), F32), (frozen.shape, F32)]
        + outgoing,
        (6 * near_rows * points, 12 << 20),
        me, send_list, states.reshape(rows, points), neighbours, weights, potential.reshape(1, points), frozen,
        scalars=1,
        remote=6,
        scratch=[
            pltpu.VMEM(send_list.shape, jnp.int32),
            pltpu.VMEM(neighbours.shape, jnp.int32),
            pltpu.VMEM(weights.shape, F32),
            pltpu.VMEM((1, points), F32),
            pltpu.SemaphoreType.DMA((6,)),
        ],
    )
    if len(pieces) == bands - 1:
        pieces = [own_frozen, *pieces]
    wide_high, wide_low, turned_high, turned_low, partial, *sent = call(
        functools.partial(start_kernel, len(pieces)),
        [((2 * columns, points), BF16)] * 2 + [((points, 2 * columns), BF16)] * 2 + [(sum_shape, F32)] + outgoing,
        (6 * rows * points * 2 * columns, 4 << 20),
        *pieces, field, *sent,
    )
    sent[0], field, diagonal, targets = lax.optimization_barrier((sent[0], field, diagonal, targets))
    total, term = field, field
    for order in range(1, TERMS + 1):
        *early, late = sent
        if paired:
            early = [swap(block, bits, parts) for block, bits in zip(early, relations[1:], strict=False)]
        else:
            early = [move(block, offset, parts) for block, offset in zip(early, relations[1:], strict=False)]
        near = [term, select, near_high, near_low, diagonal]
        if order == 1:
            base, early_high, early_low, first_high, first_low = call(
                functools.partial(near_kernel, near_rows),
                [((rows, points), F32)] + [((early_rows, points), BF16)] * 2 + [((first_rows, points), BF16)] * 2,
                (6 * rows * points * near_rows, 16 << 20),
                *near, targets, values,
            )
        else:
            (base,) = call(
                functools.partial(near_kernel, None),
                [((rows, points), F32)],
                (6 * rows * points * near_rows, 16 << 20),
                *near,
            )
        if paired:
            late = jnp.concatenate([late] + [block[None, rows:] for block in early], axis=0)
            late, base, targets = lax.optimization_barrier((late, base, targets))
            late = swap(late, 1, parts)
        else:
            late = jnp.stack([move(late[at], offset, parts) for at, offset in enumerate(relations[1 + EARLY :])])
        if order == 1:
            rest_high, rest_low = call(
                functools.partial(ghost_kernel, near_rows + early_rows + first_rows),
                [((rest_rows, points), BF16)] * 2,
                (6 * rest_rows * points, 12 << 20),
                targets, values,
            )
        base, sums = call(
            early_kernel,
            [((rows, points), F32), (sum_shape, F32)],
            (6 * rows * points * early_rows, 4 << 20),
            base, partial, early_high, early_low, *early,
        )
        last = order == TERMS
        shapes = [((rows, points), F32)]
        if not last:
            shapes += [((rows, points), F32), (sum_shape, F32)] + outgoing
        outs = call(
            functools.partial(late_kernel, order, last),
            shapes,
            (6 * rows * points * (first_rows + rest_rows), 12 << 20),
            late, base, sums, total, select, first_high, first_low, rest_high, rest_low,
            wide_high, wide_low, turned_high, turned_low,
        )
        total = outs[0]
        if not last:
            _, term, partial, *sent = outs
    return total.reshape(states.shape)


def solution(mesh):
    return jax.shard_map(
        body,
        mesh=mesh,
        in_specs=(
            P(None, "band", "mesh"),
            P(None, "band", "mesh"),
            P(None, "mesh"),
            P("mesh"),
            P("mesh", None, None),
            P(None, "mesh"),
        ),
        out_specs=P(None, "band", "mesh"),
        check_vma=False,
    )
```

```python
import functools

import jax
import jax.numpy as jnp
from jax import lax
from jax.experimental import pallas as pl
from jax.experimental.pallas import tpu as pltpu
from jax.sharding import PartitionSpec as P

TERMS = 4
REACH = 3
LANES = 128
TILE = 256

time_step = 0.3

F32, BF16 = jnp.float32, jnp.bfloat16
VMEM_LIMIT = 24 << 20


def split(value):
    high = value.astype(BF16)
    return high, (value - high.astype(F32)).astype(BF16)


def stacked(value):
    high, low = split(value)
    return jnp.concatenate([high, low], axis=0), high


def dot(left, right):
    return lax.dot_general(left, right, (((1,), (0,)), ((), ())), preferred_element_type=F32)


def product(both, high, right_high, right_low):
    rows = high.shape[0]
    result = dot(both, right_high)
    return result[:rows] + result[rows:] + dot(high, right_low)


def blocks_of(parts):
    if parts == 8:
        return [0, 1, 6, 4, 2, 7, 5, 3]
    relative = [0]
    for offset in [*range(1, REACH + 1), *range(-REACH, 0), parts // 2]:
        if offset % parts not in relative:
            relative.append(offset % parts)
    return relative


EARLY = 4
LATE_FIRST = 1


def receiver_of(me, block, parts):
    return me ^ block if parts == 8 else lax.rem(me + block, parts)


def place_of(sender, me, parts):
    relative = sender ^ me if parts == 8 else lax.rem(me - sender + parts, parts)
    result = jnp.zeros_like(relative)
    for place, block in enumerate(blocks_of(parts)):
        result = jnp.where(relative == block, place, result)
    return result


def call(kernel, out_shape, cost, *args, scalars=0, remote=0, scratch=()):
    held = slice(scalars, scalars + remote)
    args = list(args)
    args[held] = [pltpu.with_memory_space_constraint(arg, pltpu.HBM) for arg in args[held]]
    spaces = [pltpu.SMEM] * scalars + [pltpu.HBM] * remote + [pltpu.VMEM] * (len(args) - scalars - remote)
    return pl.pallas_call(
        kernel,
        out_shape=[jax.ShapeDtypeStruct(shape, dtype) for shape, dtype in out_shape],
        in_specs=[pl.BlockSpec(memory_space=space) for space in spaces],
        out_specs=[pl.BlockSpec(memory_space=pltpu.VMEM)] * len(out_shape),
        scratch_shapes=scratch,
        compiler_params=pltpu.CompilerParams(vmem_limit_bytes=VMEM_LIMIT),
        cost_estimate=pl.CostEstimate(flops=cost[0], bytes_accessed=cost[1], transcendentals=0),
    )(*args)


def stencil_rows(targets, values, outs, first):
    tall, chunk = 16, 2 * LANES
    points = targets[0].shape[1]
    row_id = lax.broadcasted_iota(jnp.int32, (tall, chunk), 0).astype(jnp.int16)
    zero = jnp.zeros((tall, chunk), BF16)
    for lane in range(0, points, chunk):
        at = [jnp.broadcast_to(t[:, lane : lane + chunk], (tall, chunk)).astype(jnp.int16) for t in targets]
        pieces = [split(jnp.broadcast_to(v[:, lane : lane + chunk], (tall, chunk))) for v in values]
        base = first
        for high_ref, low_ref in outs:

            @pl.loop(0, high_ref.shape[0] // TILE)
            def _(tile, base=base, high_ref=high_ref, low_ref=low_ref):
                start = (base + tile * TILE).astype(jnp.int16)
                local = [a - start for a in at]
                for row in range(0, TILE, tall):
                    here = row_id + jnp.int16(row)
                    high, low = zero, zero
                    for target, (value_high, value_low) in zip(local, pieces, strict=True):
                        hit = target == here
                        high = jnp.where(hit, value_high, high)
                        low = jnp.where(hit, value_low, low)
                    place = pl.multiple_of(tile * TILE + row, tall)
                    high_ref[pl.ds(place, tall), lane : lane + chunk] = high
                    low_ref[pl.ds(place, tall), lane : lane + chunk] = low

            base = base + high_ref.shape[0]


def plan_kernel(parts, tall, me_ref, *refs):
    sources, refs = refs[:6], refs[6:]
    targets_ref, values_ref, diagonal_ref, select_ref, near_high, near_low, field_ref, frozen_ref, *refs = refs
    out, (routes_ref, neighbours_ref, weights_ref, potential_ref, arrival) = refs[:-5], refs[-5:]
    arrays = [routes_ref, field_ref, neighbours_ref, weights_ref, potential_ref, frozen_ref]
    copies = [
        pltpu.make_async_copy(source, array, arrival.at[at])
        for at, (source, array) in enumerate(zip(sources, arrays, strict=True))
    ]
    for copy in copies:
        copy.start()
    count, points = neighbours_ref.shape
    capacity = routes_ref.shape[2]
    rows = field_ref.shape[0]
    me = me_ref[0]
    copies[0].wait()
    copies[1].wait()
    step = 16
    row_id = lax.broadcasted_iota(jnp.int32, (step, capacity), 0).astype(jnp.int16)
    one, zero = jnp.ones((step, capacity), BF16), jnp.zeros((step, capacity), BF16)
    for place, block in enumerate(blocks_of(parts)):
        route = routes_ref[0, pl.ds(receiver_of(me, block, parts), 1), :]
        route = jnp.broadcast_to(route, (step, capacity)).astype(jnp.int16)
        for row in range(0, points, step):
            hit = route == row_id + jnp.int16(row)
            select_ref[row : row + step, pl.ds(place * capacity, capacity)] = jnp.where(hit, one, zero)
    both, _ = stacked(field_ref[...])
    pack(both, select_ref, tall, out)
    for copy in copies[2:]:
        copy.wait()
    named = neighbours_ref[...]
    ghost = jnp.maximum(named - points, 0)
    sender = ghost // capacity
    place = place_of(sender, me, parts)
    named = jnp.where(named < points, named, points + place * capacity + (ghost - sender * capacity))
    half = 0.5 * weights_ref[...]
    diagonal_ref[...] = jnp.sum(half, axis=0, keepdims=True) + potential_ref[...]
    targets = [named[k : k + 1] for k in range(count)]
    values = [half[k : k + 1] for k in range(count)]
    for k in range(count):
        for later in range(k + 1, count):
            same = targets[k] == targets[later]
            values[k] = jnp.where(same, values[k] + values[later], values[k])
            targets[later] = jnp.where(same, -1, targets[later])
    for k in range(count):
        targets_ref[k : k + 1] = targets[k]
        values_ref[k : k + 1] = values[k]
    stencil_rows(targets, values, [(near_high, near_low)], 0)


def ghost_kernel(first, targets_ref, values_ref, *outs):
    count = targets_ref.shape[0]
    targets = [targets_ref[k : k + 1] for k in range(count)]
    values = [values_ref[k : k + 1] for k in range(count)]
    stencil_rows(targets, values, list(zip(outs[::2], outs[1::2], strict=True)), first)


def intersect(both, turned):
    rows = both.shape[0] // 2
    half = rows // 2
    columns = turned.shape[1] // 4
    result = dot(both, turned)
    result = result[:rows, : 2 * columns] + result[rows:, : 2 * columns] + result[:rows, 2 * columns :]
    if columns >= LANES:
        return result[:half, :columns] + result[half:, columns:]
    result = result[:half] + pltpu.roll(result[half:], columns, 1)
    lane = lax.broadcasted_iota(jnp.int32, (half // 2, LANES), 1)
    return jnp.where(lane < columns, result[: half // 2], pltpu.roll(result[half // 2 :], columns, 1))


def exchange_term(sums, wide):
    columns = wide.shape[0] // 4
    if columns >= LANES:
        zero = jnp.zeros_like(sums)
        left = jnp.concatenate([jnp.concatenate([sums, zero], axis=1), jnp.concatenate([zero, sums], axis=1)], axis=0)
    else:
        lower = lax.broadcasted_iota(jnp.int32, sums.shape, 1) < columns
        rolled = pltpu.roll(sums, columns, 1)
        left = jnp.concatenate(
            [
                jnp.where(lower, sums, 0.0),
                jnp.where(lower, rolled, 0.0),
                jnp.where(lower, 0.0, rolled),
                jnp.where(lower, 0.0, sums),
            ],
            axis=0,
        )
    rows = left.shape[0]
    high, low = split(left)
    upper = jnp.concatenate([high, high], axis=1)
    lower = jnp.concatenate([low, jnp.zeros_like(low)], axis=1)
    result = dot(jnp.concatenate([upper, lower], axis=0), wide)
    return result[:rows] + result[rows:]


def slots_of(rows, tall, refs):
    slots = [(ref, 0) for ref in refs[: EARLY - 1]]
    if refs[0].shape[0] > rows + tall:
        return slots + [(ref, rows + tall) for ref in refs[: EARLY - 1]]
    return slots + [(refs[-1].at[at], tall) for at in range(refs[-1].shape[0])]


def packed(both, select_ref, place):
    rows = both.shape[0] // 2
    result = dot(both, select_ref[:, pl.ds(place * TILE, TILE)])
    return result[:rows] + result[rows:]


def pack(both, select_ref, tall, refs):
    rows = both.shape[0] // 2
    for place, (ref, start) in enumerate(slots_of(rows, tall, refs)):
        ref[start : start + rows, :] = packed(both, select_ref, place + 2)


def widened(partial, capacity):
    tall, width = partial.shape
    if width == capacity:
        return partial
    return jnp.concatenate([partial, jnp.zeros((tall, capacity - width), F32)], axis=1)


def spread(partial, rows, refs):
    tall = partial.shape[0]
    partial = widened(partial, refs[0].shape[1])
    for ref in refs[: EARLY - 1]:
        ref[rows : rows + tall, :] = partial
    for late_ref in refs[EARLY - 1 :]:
        for at in range(late_ref.shape[0]):
            late_ref[at, :tall, :] = partial


def start_kernel(groups, *refs):
    pieces, (field_ref, *refs) = refs[:groups], refs[groups:]
    sent = (len(refs) - 3) // 2
    ready, (wide_ref, turned_ref, partial_ref, *out) = refs[:sent], refs[sent:]
    rows = field_ref.shape[0]
    pieces = [piece[...] for piece in pieces]
    if pieces[0].ndim == 4:
        pieces = [pieces[0][band] for band in range(pieces[0].shape[0])]
    real = jnp.concatenate([piece[0] for piece in pieces], axis=0)
    imag = jnp.concatenate([piece[1] for piece in pieces], axis=0)
    wide = jnp.concatenate([real, -imag, imag, real], axis=0)
    wide_ref[...] = jnp.concatenate(split(wide), axis=0)
    turned_ref[...] = jnp.concatenate(split(wide.T), axis=1)
    both, _ = stacked(field_ref[...])
    partial = intersect(both, turned_ref[...])
    partial_ref[...] = partial
    tall = partial.shape[0]
    for (source, start), (target, _) in zip(slots_of(rows, tall, ready), slots_of(rows, tall, out), strict=True):
        target[start : start + rows, :] = source[start : start + rows, :]
    spread(partial, rows, out)


def near_kernel(first, term_ref, partial_ref, select_ref, near_high, near_low, diagonal_ref, *refs):
    if first is not None:
        targets_ref, values_ref, base_ref, message_ref, *outs = refs
        ghost_kernel(first, targets_ref, values_ref, *outs)
    else:
        base_ref, message_ref = refs
    rows, points = term_ref.shape
    term = term_ref[...]
    both, high = stacked(term)
    message_ref[:rows, :] = packed(both, select_ref, 1)
    message_ref[rows:, :] = widened(partial_ref[...], message_ref.shape[1])
    own_both, own_high = stacked(packed(both, select_ref, 0))
    both = jnp.concatenate([both, own_both], axis=1)
    high = jnp.concatenate([high, own_high], axis=1)
    base_ref[...] = term * diagonal_ref[...] - product(both, high, near_high[...], near_low[...])


def ghost_values(blocks, high, low):
    pieces = [stacked(block) for block in blocks]
    both = jnp.concatenate([piece[0] for piece in pieces], axis=1)
    return product(both, jnp.concatenate([piece[1] for piece in pieces], axis=1), high, low)


def early_kernel(base_ref, partial_ref, early_high, early_low, *refs):
    early_refs, (base_out, sums_out) = refs[:-2], refs[-2:]
    rows = base_ref.shape[0]
    sums = partial_ref[...]
    tall, width = sums.shape
    for ref in early_refs:
        sums = sums + ref[rows : rows + tall, :width]
    sums_out[...] = sums
    base_out[...] = base_ref[...] - ghost_values([ref[:rows, :] for ref in early_refs], early_high[...], early_low[...])


def late_kernel(order, last, late_ref, base_ref, sums_ref, total_ref, select_ref, first_high, first_low, rest_high, rest_low, wide_ref, turned_ref, *outs):
    half = base_ref.shape[0] // 2
    blocks = range(late_ref.shape[0])
    sums = sums_ref[...]
    tall, width = sums.shape
    for block in blocks:
        sums = sums + late_ref[block, :tall, :width]
    ghosts = [late_ref[block, tall:, :] for block in blocks]
    cut = first_high.shape[0] // late_ref.shape[2]
    image = base_ref[...] - exchange_term(sums, wide_ref[...])
    image = image - ghost_values(ghosts[:cut], first_high[...], first_low[...])
    image = image - ghost_values(ghosts[cut:], rest_high[...], rest_low[...])
    scale = time_step / order
    term = jnp.concatenate([scale * image[half:], -scale * image[:half]], axis=0)
    outs[0][...] = total_ref[...] + term
    if last:
        return
    _, term_ref, partial_ref, *out = outs
    term_ref[...] = term
    both, _ = stacked(term)
    partial = intersect(both, turned_ref[...])
    partial_ref[...] = partial
    pack(both, select_ref, tall, out)
    spread(partial, term.shape[0], out)


def swap(value, bits, parts):
    return lax.ppermute(value, "mesh", [(part, part ^ bits) for part in range(parts)])


def move(value, offset, parts):
    return lax.ppermute(value, "mesh", [(part, (part + offset) % parts) for part in range(parts)])


def gather_frozen(frozen):
    bands = lax.axis_size("band")
    if bands <= 4:
        return [lax.ppermute(frozen, "band", [(at, (at + step) % bands) for at in range(bands)]) for step in range(1, bands)]
    return [lax.all_gather(frozen, "band", axis=0, tiled=False)]


def body(states, frozen, weights, potential, send_list, neighbours):
    parts = lax.axis_size("mesh")
    points = states.shape[2]
    rows = 2 * states.shape[1]
    half = rows // 2
    capacity = send_list.shape[2]
    relations = blocks_of(parts)
    places = len(relations)
    paired = parts == 8
    me = lax.axis_index("mesh").astype(jnp.int32).reshape(1)
    count = neighbours.shape[0]

    bands = lax.axis_size("band")
    pieces = gather_frozen(frozen)
    columns = 2 * bands * frozen.shape[1]
    sum_shape = (half, columns) if columns >= LANES else (half * columns // LANES, LANES)
    tall = rows + sum_shape[0]
    late_blocks = places - 1 - EARLY
    outgoing = [((tall + rows if paired else tall, capacity), F32)] * (EARLY - 1)
    if not paired:
        outgoing += [((late_blocks, tall, capacity), F32)]
    near_rows, early_rows = points + capacity, EARLY * capacity
    first_rows = LATE_FIRST * capacity
    rest_rows = late_blocks * capacity - first_rows
    targets, values, diagonal, select, near_high, near_low, field, own_frozen, *sent = call(
        functools.partial(plan_kernel, parts, sum_shape[0]),
        [((count, points), jnp.int32), ((count, points), F32), ((1, points), F32), ((points, places * capacity), BF16)]
        + [((near_rows, points), BF16)] * 2
        + [((rows, points), F32), (frozen.shape, F32)]
        + outgoing,
        (6 * near_rows * points, 12 << 20),
        me, send_list, states.reshape(rows, points), neighbours, weights, potential.reshape(1, points), frozen,
        scalars=1,
        remote=6,
        scratch=[
            pltpu.VMEM(send_list.shape, jnp.int32),
            pltpu.VMEM(neighbours.shape, jnp.int32),
            pltpu.VMEM(weights.shape, F32),
            pltpu.VMEM((1, points), F32),
            pltpu.SemaphoreType.DMA((6,)),
        ],
    )
    if len(pieces) == bands - 1:
        pieces = [own_frozen, *pieces]
    wide, turned, partial, *sent = call(
        functools.partial(start_kernel, len(pieces)),
        [((4 * columns, points), BF16), ((points, 4 * columns), BF16), (sum_shape, F32)] + outgoing,
        (6 * rows * points * 2 * columns, 4 << 20),
        *pieces, field, *sent,
    )
    sent[0], field, diagonal, targets = lax.optimization_barrier((sent[0], field, diagonal, targets))
    total, term = field, field
    for order in range(1, TERMS + 1):
        if paired:
            early = [swap(block, bits, parts) for block, bits in zip(sent, relations[2:], strict=False)]
        else:
            early = [move(block, offset, parts) for block, offset in zip(sent[: EARLY - 1], relations[2:], strict=False)]
        near = [term, partial, select, near_high, near_low, diagonal]
        if order == 1:
            base, message, early_high, early_low, first_high, first_low = call(
                functools.partial(near_kernel, near_rows),
                [((rows, points), F32), ((tall, capacity), F32)] + [((early_rows, points), BF16)] * 2 + [((first_rows, points), BF16)] * 2,
                (6 * rows * points * near_rows, 16 << 20),
                *near, targets, values,
            )
        else:
            base, message = call(
                functools.partial(near_kernel, None),
                [((rows, points), F32), ((tall, capacity), F32)],
                (6 * rows * points * near_rows, 16 << 20),
                *near,
            )
        if paired:
            message = swap(message, 1, parts)
            late = jnp.stack([block[rows:] for block in early])
            if order == 1:
                late, base, targets = lax.optimization_barrier((late, base, targets))
            else:
                late, message, base, near_high, near_low, diagonal = lax.optimization_barrier(
                    (late, message, base, near_high, near_low, diagonal)
                )
            late = swap(late, 1, parts)
        else:
            message = move(message, relations[1], parts)
            late = jnp.stack([move(sent[-1][at], offset, parts) for at, offset in enumerate(relations[1 + EARLY :])])
        if order == 1:
            rest_high, rest_low = call(
                functools.partial(ghost_kernel, near_rows + early_rows + first_rows),
                [((rest_rows, points), BF16)] * 2,
                (6 * rest_rows * points, 12 << 20),
                targets, values,
            )
        base, sums = call(
            early_kernel,
            [((rows, points), F32), (sum_shape, F32)],
            (6 * rows * points * early_rows, 4 << 20),
            base, partial, early_high, early_low, message, *early,
        )
        last = order == TERMS
        shapes = [((rows, points), F32)]
        if not last:
            shapes += [((rows, points), F32), (sum_shape, F32)] + outgoing
        outs = call(
            functools.partial(late_kernel, order, last),
            shapes,
            (6 * rows * points * (first_rows + rest_rows), 12 << 20),
            late, base, sums, total, select, first_high, first_low, rest_high, rest_low,
            wide, turned,
        )
        total = outs[0]
        if not last:
            _, term, partial, *sent = outs
    return total.reshape(states.shape)


def solution(mesh):
    return jax.shard_map(
        body,
        mesh=mesh,
        in_specs=(
            P(None, "band", "mesh"),
            P(None, "band", "mesh"),
            P(None, "mesh"),
            P("mesh"),
            P("mesh", None, None),
            P(None, "mesh"),
        ),
        out_specs=P(None, "band", "mesh"),
        check_vma=False,
    )
```

```python
import functools

import jax
import jax.numpy as jnp
from jax import lax
from jax.experimental import pallas as pl
from jax.experimental.pallas import tpu as pltpu
from jax.sharding import PartitionSpec as P

TERMS = 4
REACH = 3
LANES = 128
TILE = 256

time_step = 0.3

F32, BF16 = jnp.float32, jnp.bfloat16
VMEM_LIMIT = 24 << 20


def split(value):
    high = value.astype(BF16)
    return high, (value - high.astype(F32)).astype(BF16)


def stacked(value):
    high, low = split(value)
    return jnp.concatenate([high, low], axis=0), high


def dot(left, right):
    return lax.dot_general(left, right, (((1,), (0,)), ((), ())), preferred_element_type=F32)


def product(both, high, right_high, right_low):
    rows = high.shape[0]
    result = dot(both, right_high)
    return result[:rows] + result[rows:] + dot(high, right_low)


def blocks_of(parts):
    if parts == 8:
        return [0, 1, 6, 4, 2, 7, 5, 3]
    relative = [0]
    for offset in [*range(1, REACH + 1), *range(-REACH, 0), parts // 2]:
        if offset % parts not in relative:
            relative.append(offset % parts)
    return relative


EARLY = 4
LATE_FIRST = 1


def receiver_of(me, block, parts):
    return me ^ block if parts == 8 else lax.rem(me + block, parts)


def place_of(sender, me, parts):
    relative = sender ^ me if parts == 8 else lax.rem(me - sender + parts, parts)
    result = jnp.zeros_like(relative)
    for place, block in enumerate(blocks_of(parts)):
        result = jnp.where(relative == block, place, result)
    return result


def call(kernel, out_shape, cost, *args, scalars=0, remote=0, scratch=()):
    held = slice(scalars, scalars + remote)
    args = list(args)
    args[held] = [pltpu.with_memory_space_constraint(arg, pltpu.HBM) for arg in args[held]]
    spaces = [pltpu.SMEM] * scalars + [pltpu.HBM] * remote + [pltpu.VMEM] * (len(args) - scalars - remote)
    return pl.pallas_call(
        kernel,
        out_shape=[jax.ShapeDtypeStruct(shape, dtype) for shape, dtype in out_shape],
        in_specs=[pl.BlockSpec(memory_space=space) for space in spaces],
        out_specs=[pl.BlockSpec(memory_space=pltpu.VMEM)] * len(out_shape),
        scratch_shapes=scratch,
        compiler_params=pltpu.CompilerParams(vmem_limit_bytes=VMEM_LIMIT),
        cost_estimate=pl.CostEstimate(flops=cost[0], bytes_accessed=cost[1], transcendentals=0),
    )(*args)


def stencil_rows(targets, values, outs, first):
    tall, chunk = 16, 2 * LANES
    points = targets[0].shape[1]
    row_id = lax.broadcasted_iota(jnp.int32, (tall, chunk), 0).astype(jnp.int16)
    zero = jnp.zeros((tall, chunk), BF16)
    for lane in range(0, points, chunk):
        at = [jnp.broadcast_to(t[:, lane : lane + chunk], (tall, chunk)).astype(jnp.int16) for t in targets]
        pieces = [split(jnp.broadcast_to(v[:, lane : lane + chunk], (tall, chunk))) for v in values]
        base = first
        for high_ref, low_ref in outs:

            @pl.loop(0, high_ref.shape[0] // TILE)
            def _(tile, base=base, high_ref=high_ref, low_ref=low_ref):
                start = (base + tile * TILE).astype(jnp.int16)
                local = [a - start for a in at]
                for row in range(0, TILE, tall):
                    here = row_id + jnp.int16(row)
                    high, low = zero, zero
                    for target, (value_high, value_low) in zip(local, pieces, strict=True):
                        hit = target == here
                        high = jnp.where(hit, value_high, high)
                        low = jnp.where(hit, value_low, low)
                    place = pl.multiple_of(tile * TILE + row, tall)
                    high_ref[pl.ds(place, tall), lane : lane + chunk] = high
                    low_ref[pl.ds(place, tall), lane : lane + chunk] = low

            base = base + high_ref.shape[0]


def plan_kernel(parts, tall, me_ref, *refs):
    sources, refs = refs[:6], refs[6:]
    targets_ref, values_ref, diagonal_ref, select_ref, near_high, near_low, field_ref, frozen_ref, *refs = refs
    out, (routes_ref, neighbours_ref, weights_ref, potential_ref, arrival) = refs[:-5], refs[-5:]
    arrays = [routes_ref, field_ref, neighbours_ref, weights_ref, potential_ref, frozen_ref]
    copies = [
        pltpu.make_async_copy(source, array, arrival.at[at])
        for at, (source, array) in enumerate(zip(sources, arrays, strict=True))
    ]
    for copy in copies:
        copy.start()
    count, points = neighbours_ref.shape
    capacity = routes_ref.shape[2]
    rows = field_ref.shape[0]
    me = me_ref[0]
    copies[0].wait()
    copies[1].wait()
    step = 16
    row_id = lax.broadcasted_iota(jnp.int32, (step, capacity), 0).astype(jnp.int16)
    one, zero = jnp.ones((step, capacity), BF16), jnp.zeros((step, capacity), BF16)
    for place, block in enumerate(blocks_of(parts)):
        route = routes_ref[0, pl.ds(receiver_of(me, block, parts), 1), :]
        route = jnp.broadcast_to(route, (step, capacity)).astype(jnp.int16)
        for row in range(0, points, step):
            hit = route == row_id + jnp.int16(row)
            select_ref[row : row + step, pl.ds(place * capacity, capacity)] = jnp.where(hit, one, zero)
    both, _ = stacked(field_ref[...])
    pack(both, select_ref, tall, out)
    for copy in copies[2:]:
        copy.wait()
    named = neighbours_ref[...]
    ghost = jnp.maximum(named - points, 0)
    sender = ghost // capacity
    place = place_of(sender, me, parts)
    named = jnp.where(named < points, named, points + place * capacity + (ghost - sender * capacity))
    half = 0.5 * weights_ref[...]
    diagonal_ref[...] = jnp.sum(half, axis=0, keepdims=True) + potential_ref[...]
    targets = [named[k : k + 1] for k in range(count)]
    values = [half[k : k + 1] for k in range(count)]
    for k in range(count):
        for later in range(k + 1, count):
            same = targets[k] == targets[later]
            values[k] = jnp.where(same, values[k] + values[later], values[k])
            targets[later] = jnp.where(same, -1, targets[later])
    for k in range(count):
        targets_ref[k : k + 1] = targets[k]
        values_ref[k : k + 1] = values[k]
    stencil_rows(targets, values, [(near_high, near_low)], 0)


def ghost_kernel(first, targets_ref, values_ref, *outs):
    count = targets_ref.shape[0]
    targets = [targets_ref[k : k + 1] for k in range(count)]
    values = [values_ref[k : k + 1] for k in range(count)]
    stencil_rows(targets, values, list(zip(outs[::2], outs[1::2], strict=True)), first)


def intersect(both, turned):
    rows = both.shape[0] // 2
    half = rows // 2
    columns = turned.shape[1] // 4
    result = dot(both, turned)
    result = result[:rows, : 2 * columns] + result[rows:, : 2 * columns] + result[:rows, 2 * columns :]
    if columns >= LANES:
        return result[:half, :columns] + result[half:, columns:]
    result = result[:half] + pltpu.roll(result[half:], columns, 1)
    lane = lax.broadcasted_iota(jnp.int32, (half // 2, LANES), 1)
    return jnp.where(lane < columns, result[: half // 2], pltpu.roll(result[half // 2 :], columns, 1))


def exchange_term(sums, wide):
    columns = wide.shape[0] // 4
    if columns >= LANES:
        zero = jnp.zeros_like(sums)
        left = jnp.concatenate([jnp.concatenate([sums, zero], axis=1), jnp.concatenate([zero, sums], axis=1)], axis=0)
    else:
        lower = lax.broadcasted_iota(jnp.int32, sums.shape, 1) < columns
        rolled = pltpu.roll(sums, columns, 1)
        left = jnp.concatenate(
            [
                jnp.where(lower, sums, 0.0),
                jnp.where(lower, rolled, 0.0),
                jnp.where(lower, 0.0, rolled),
                jnp.where(lower, 0.0, sums),
            ],
            axis=0,
        )
    rows = left.shape[0]
    high, low = split(left)
    upper = jnp.concatenate([high, high], axis=1)
    lower = jnp.concatenate([low, jnp.zeros_like(low)], axis=1)
    result = dot(jnp.concatenate([upper, lower], axis=0), wide)
    return result[:rows] + result[rows:]


def slots_of(rows, tall, refs):
    slots = [(ref, 0) for ref in refs[: EARLY - 1]]
    if refs[0].shape[0] > rows + tall:
        return slots + [(ref, rows + tall) for ref in refs[: EARLY - 1]]
    return slots + [(refs[-1].at[at], tall) for at in range(refs[-1].shape[0])]


def packed(both, select_ref, place):
    rows = both.shape[0] // 2
    result = dot(both, select_ref[:, pl.ds(place * TILE, TILE)])
    return result[:rows] + result[rows:]


def pack(both, select_ref, tall, refs):
    rows = both.shape[0] // 2
    for place, (ref, start) in enumerate(slots_of(rows, tall, refs)):
        ref[start : start + rows, :] = packed(both, select_ref, place + 2)


def widened(partial, capacity):
    tall, width = partial.shape
    if width == capacity:
        return partial
    return jnp.concatenate([partial, jnp.zeros((tall, capacity - width), F32)], axis=1)


def spread(partial, rows, refs):
    tall = partial.shape[0]
    partial = widened(partial, refs[0].shape[1])
    for ref in refs[: EARLY - 1]:
        ref[rows : rows + tall, :] = partial
    for late_ref in refs[EARLY - 1 :]:
        for at in range(late_ref.shape[0]):
            late_ref[at, :tall, :] = partial


def start_kernel(groups, *refs):
    pieces, (field_ref, *refs) = refs[:groups], refs[groups:]
    sent = (len(refs) - 3) // 2
    ready, (wide_ref, turned_ref, partial_ref, *out) = refs[:sent], refs[sent:]
    rows = field_ref.shape[0]
    pieces = [piece[...] for piece in pieces]
    if pieces[0].ndim == 4:
        pieces = [pieces[0][band] for band in range(pieces[0].shape[0])]
    real = jnp.concatenate([piece[0] for piece in pieces], axis=0)
    imag = jnp.concatenate([piece[1] for piece in pieces], axis=0)
    wide = jnp.concatenate([real, -imag, imag, real], axis=0)
    wide_ref[...] = jnp.concatenate(split(wide), axis=0)
    turned_ref[...] = jnp.concatenate(split(wide.T), axis=1)
    both, _ = stacked(field_ref[...])
    partial = intersect(both, turned_ref[...])
    partial_ref[...] = partial
    tall = partial.shape[0]
    for (source, start), (target, _) in zip(slots_of(rows, tall, ready), slots_of(rows, tall, out), strict=True):
        target[start : start + rows, :] = source[start : start + rows, :]
    spread(partial, rows, out)


def near_kernel(first, term_ref, partial_ref, select_ref, near_high, near_low, diagonal_ref, *refs):
    if first is not None:
        targets_ref, values_ref, base_ref, message_ref, *outs = refs
        ghost_kernel(first, targets_ref, values_ref, *outs)
    else:
        base_ref, message_ref = refs
    rows, points = term_ref.shape
    term = term_ref[...]
    both, high = stacked(term)
    message_ref[:rows, :] = packed(both, select_ref, 1)
    message_ref[rows:, :] = widened(partial_ref[...], message_ref.shape[1])
    own_both, own_high = stacked(packed(both, select_ref, 0))
    both = jnp.concatenate([both, own_both], axis=1)
    high = jnp.concatenate([high, own_high], axis=1)
    base_ref[...] = term * diagonal_ref[...] - product(both, high, near_high[...], near_low[...])


def ghost_values(blocks, high, low):
    pieces = [stacked(block) for block in blocks]
    both = jnp.concatenate([piece[0] for piece in pieces], axis=1)
    return product(both, jnp.concatenate([piece[1] for piece in pieces], axis=1), high, low)


def early_kernel(base_ref, partial_ref, early_high, early_low, *refs):
    early_refs, (base_out, sums_out) = refs[:-2], refs[-2:]
    rows = base_ref.shape[0]
    sums = partial_ref[...]
    tall, width = sums.shape
    for ref in early_refs:
        sums = sums + ref[rows : rows + tall, :width]
    sums_out[...] = sums
    base_out[...] = base_ref[...] - ghost_values([ref[:rows, :] for ref in early_refs], early_high[...], early_low[...])


def late_kernel(order, last, late_ref, base_ref, sums_ref, total_ref, select_ref, first_high, first_low, rest_high, rest_low, wide_ref, turned_ref, *outs):
    half = base_ref.shape[0] // 2
    blocks = range(late_ref.shape[0])
    sums = sums_ref[...]
    tall, width = sums.shape
    for block in blocks:
        sums = sums + late_ref[block, :tall, :width]
    ghosts = [late_ref[block, tall:, :] for block in blocks]
    cut = first_high.shape[0] // late_ref.shape[2]
    image = base_ref[...] - exchange_term(sums, wide_ref[...])
    image = image - ghost_values(ghosts[:cut], first_high[...], first_low[...])
    image = image - ghost_values(ghosts[cut:], rest_high[...], rest_low[...])
    scale = time_step / order
    term = jnp.concatenate([scale * image[half:], -scale * image[:half]], axis=0)
    outs[0][...] = total_ref[...] + term
    if last:
        return
    _, term_ref, partial_ref, *out = outs
    term_ref[...] = term
    both, _ = stacked(term)
    partial = intersect(both, turned_ref[...])
    partial_ref[...] = partial
    pack(both, select_ref, tall, out)
    spread(partial, term.shape[0], out)


def swap(value, bits, parts):
    return lax.ppermute(value, "mesh", [(part, part ^ bits) for part in range(parts)])


def move(value, offset, parts):
    return lax.ppermute(value, "mesh", [(part, (part + offset) % parts) for part in range(parts)])


def gather_frozen(frozen):
    bands = lax.axis_size("band")
    if bands == 4:
        return [lax.ppermute(frozen, "band", [(at, at ^ step) for at in range(bands)]) for step in (2, 1, 3)]
    return [lax.all_gather(frozen, "band", axis=0, tiled=False)]


def body(states, frozen, weights, potential, send_list, neighbours):
    parts = lax.axis_size("mesh")
    points = states.shape[2]
    rows = 2 * states.shape[1]
    half = rows // 2
    capacity = send_list.shape[2]
    relations = blocks_of(parts)
    places = len(relations)
    paired = parts == 8
    me = lax.axis_index("mesh").astype(jnp.int32).reshape(1)
    count = neighbours.shape[0]

    bands = lax.axis_size("band")
    pieces = gather_frozen(frozen)
    columns = 2 * bands * frozen.shape[1]
    sum_shape = (half, columns) if columns >= LANES else (half * columns // LANES, LANES)
    tall = rows + sum_shape[0]
    late_blocks = places - 1 - EARLY
    outgoing = [((tall + rows if paired else tall, capacity), F32)] * (EARLY - 1)
    if not paired:
        outgoing += [((late_blocks, tall, capacity), F32)]
    near_rows, early_rows = points + capacity, EARLY * capacity
    first_rows = LATE_FIRST * capacity
    rest_rows = late_blocks * capacity - first_rows
    targets, values, diagonal, select, near_high, near_low, field, own_frozen, *sent = call(
        functools.partial(plan_kernel, parts, sum_shape[0]),
        [((count, points), jnp.int32), ((count, points), F32), ((1, points), F32), ((points, places * capacity), BF16)]
        + [((near_rows, points), BF16)] * 2
        + [((rows, points), F32), (frozen.shape, F32)]
        + outgoing,
        (6 * near_rows * points, 12 << 20),
        me, send_list, states.reshape(rows, points), neighbours, weights, potential.reshape(1, points), frozen,
        scalars=1,
        remote=6,
        scratch=[
            pltpu.VMEM(send_list.shape, jnp.int32),
            pltpu.VMEM(neighbours.shape, jnp.int32),
            pltpu.VMEM(weights.shape, F32),
            pltpu.VMEM((1, points), F32),
            pltpu.SemaphoreType.DMA((6,)),
        ],
    )
    if len(pieces) == bands - 1:
        pieces = [own_frozen, *pieces]
    wide, turned, partial, *sent = call(
        functools.partial(start_kernel, len(pieces)),
        [((4 * columns, points), BF16), ((points, 4 * columns), BF16), (sum_shape, F32)] + outgoing,
        (6 * rows * points * 2 * columns, 4 << 20),
        *pieces, field, *sent,
    )
    sent[0], field, diagonal, targets = lax.optimization_barrier((sent[0], field, diagonal, targets))
    total, term = field, field
    for order in range(1, TERMS + 1):
        if paired:
            early = [swap(block, bits, parts) for block, bits in zip(sent, relations[2:], strict=False)]
        else:
            early = [move(block, offset, parts) for block, offset in zip(sent[: EARLY - 1], relations[2:], strict=False)]
        near = [term, partial, select, near_high, near_low, diagonal]
        if order == 1:
            base, message, early_high, early_low, first_high, first_low = call(
                functools.partial(near_kernel, near_rows),
                [((rows, points), F32), ((tall, capacity), F32)] + [((early_rows, points), BF16)] * 2 + [((first_rows, points), BF16)] * 2,
                (6 * rows * points * near_rows, 16 << 20),
                *near, targets, values,
            )
        else:
            base, message = call(
                functools.partial(near_kernel, None),
                [((rows, points), F32), ((tall, capacity), F32)],
                (6 * rows * points * near_rows, 16 << 20),
                *near,
            )
        if paired:
            message = swap(message, 1, parts)
            late = jnp.stack([block[rows:] for block in early])
            if order == 1:
                late, base, targets = lax.optimization_barrier((late, base, targets))
            else:
                late, message, base, near_high, near_low, diagonal = lax.optimization_barrier(
                    (late, message, base, near_high, near_low, diagonal)
                )
            late = swap(late, 1, parts)
        else:
            message = move(message, relations[1], parts)
            late = jnp.stack([move(sent[-1][at], offset, parts) for at, offset in enumerate(relations[1 + EARLY :])])
        if order == 1:
            rest_high, rest_low = call(
                functools.partial(ghost_kernel, near_rows + early_rows + first_rows),
                [((rest_rows, points), BF16)] * 2,
                (6 * rest_rows * points, 12 << 20),
                targets, values,
            )
        base, sums = call(
            early_kernel,
            [((rows, points), F32), (sum_shape, F32)],
            (6 * rows * points * early_rows, 4 << 20),
            base, partial, early_high, early_low, message, *early,
        )
        last = order == TERMS
        shapes = [((rows, points), F32)]
        if not last:
            shapes += [((rows, points), F32), (sum_shape, F32)] + outgoing
        outs = call(
            functools.partial(late_kernel, order, last),
            shapes,
            (6 * rows * points * (first_rows + rest_rows), 12 << 20),
            late, base, sums, total, select, first_high, first_low, rest_high, rest_low,
            wide, turned,
        )
        total = outs[0]
        if not last:
            _, term, partial, *sent = outs
    return total.reshape(states.shape)


def solution(mesh):
    return jax.shard_map(
        body,
        mesh=mesh,
        in_specs=(
            P(None, "band", "mesh"),
            P(None, "band", "mesh"),
            P(None, "mesh"),
            P("mesh"),
            P("mesh", None, None),
            P(None, "mesh"),
        ),
        out_specs=P(None, "band", "mesh"),
        check_vma=False,
    )
```

```python
import functools

import jax
import jax.numpy as jnp
from jax import lax
from jax.experimental import pallas as pl
from jax.experimental.pallas import tpu as pltpu
from jax.sharding import PartitionSpec as P

TERMS = 4
REACH = 3
LANES = 128
TILE = 256

time_step = 0.3

F32, BF16 = jnp.float32, jnp.bfloat16
VMEM_LIMIT = 24 << 20


def split(value):
    high = value.astype(BF16)
    return high, (value - high.astype(F32)).astype(BF16)


def stacked(value):
    high, low = split(value)
    return jnp.concatenate([high, low], axis=0), high


def dot(left, right):
    return lax.dot_general(left, right, (((1,), (0,)), ((), ())), preferred_element_type=F32)


def product(both, high, right_high, right_low):
    rows = high.shape[0]
    result = dot(both, right_high)
    return result[:rows] + result[rows:] + dot(high, right_low)


def blocks_of(parts):
    if parts == 8:
        return [0, 1, 6, 4, 2, 7, 5, 3]
    relative = [0]
    for offset in [*range(1, REACH + 1), *range(-REACH, 0), parts // 2]:
        if offset % parts not in relative:
            relative.append(offset % parts)
    return relative


EARLY = 4
LATE_FIRST = 1


def receiver_of(me, block, parts):
    return me ^ block if parts == 8 else lax.rem(me + block, parts)


def place_of(sender, me, parts):
    relative = sender ^ me if parts == 8 else lax.rem(me - sender + parts, parts)
    result = jnp.zeros_like(relative)
    for place, block in enumerate(blocks_of(parts)):
        result = jnp.where(relative == block, place, result)
    return result


def call(kernel, out_shape, cost, *args, scalars=0, remote=0, scratch=()):
    held = slice(scalars, scalars + remote)
    args = list(args)
    args[held] = [pltpu.with_memory_space_constraint(arg, pltpu.HBM) for arg in args[held]]
    spaces = [pltpu.SMEM] * scalars + [pltpu.HBM] * remote + [pltpu.VMEM] * (len(args) - scalars - remote)
    return pl.pallas_call(
        kernel,
        out_shape=[jax.ShapeDtypeStruct(shape, dtype) for shape, dtype in out_shape],
        in_specs=[pl.BlockSpec(memory_space=space) for space in spaces],
        out_specs=[pl.BlockSpec(memory_space=pltpu.VMEM)] * len(out_shape),
        scratch_shapes=scratch,
        compiler_params=pltpu.CompilerParams(vmem_limit_bytes=VMEM_LIMIT),
        cost_estimate=pl.CostEstimate(flops=cost[0], bytes_accessed=cost[1], transcendentals=0),
    )(*args)


def stencil_rows(targets, values, outs, first):
    tall, chunk = 16, 2 * LANES
    points = targets[0].shape[1]
    row_id = lax.broadcasted_iota(jnp.int32, (tall, chunk), 0).astype(jnp.int16)
    zero = jnp.zeros((tall, chunk), BF16)
    for lane in range(0, points, chunk):
        at = [jnp.broadcast_to(t[:, lane : lane + chunk], (tall, chunk)).astype(jnp.int16) for t in targets]
        pieces = [split(jnp.broadcast_to(v[:, lane : lane + chunk], (tall, chunk))) for v in values]
        base = first
        for high_ref, low_ref in outs:

            @pl.loop(0, high_ref.shape[0] // TILE)
            def _(tile, base=base, high_ref=high_ref, low_ref=low_ref):
                start = (base + tile * TILE).astype(jnp.int16)
                local = [a - start for a in at]
                for row in range(0, TILE, tall):
                    here = row_id + jnp.int16(row)
                    high, low = zero, zero
                    for target, (value_high, value_low) in zip(local, pieces, strict=True):
                        hit = target == here
                        high = jnp.where(hit, value_high, high)
                        low = jnp.where(hit, value_low, low)
                    place = pl.multiple_of(tile * TILE + row, tall)
                    high_ref[pl.ds(place, tall), lane : lane + chunk] = high
                    low_ref[pl.ds(place, tall), lane : lane + chunk] = low

            base = base + high_ref.shape[0]


def plan_kernel(parts, tall, me_ref, *refs):
    sources, refs = refs[:6], refs[6:]
    targets_ref, values_ref, diagonal_ref, select_ref, near_high, near_low, field_ref, frozen_ref, *refs = refs
    out, (routes_ref, neighbours_ref, weights_ref, potential_ref, arrival) = refs[:-5], refs[-5:]
    arrays = [routes_ref, field_ref, neighbours_ref, weights_ref, potential_ref, frozen_ref]
    copies = [
        pltpu.make_async_copy(source, array, arrival.at[at])
        for at, (source, array) in enumerate(zip(sources, arrays, strict=True))
    ]
    for copy in copies:
        copy.start()
    count, points = neighbours_ref.shape
    capacity = routes_ref.shape[2]
    rows = field_ref.shape[0]
    me = me_ref[0]
    copies[0].wait()
    copies[1].wait()
    step = 16
    row_id = lax.broadcasted_iota(jnp.int32, (step, capacity), 0).astype(jnp.int16)
    one, zero = jnp.ones((step, capacity), BF16), jnp.zeros((step, capacity), BF16)
    for place, block in enumerate(blocks_of(parts)):
        route = routes_ref[0, pl.ds(receiver_of(me, block, parts), 1), :]
        route = jnp.broadcast_to(route, (step, capacity)).astype(jnp.int16)
        for row in range(0, points, step):
            hit = route == row_id + jnp.int16(row)
            select_ref[row : row + step, pl.ds(place * capacity, capacity)] = jnp.where(hit, one, zero)
    both, _ = stacked(field_ref[...])
    *out, message_ref = out
    pack(both, select_ref, tall, out)
    message_ref[: field_ref.shape[0], :] = packed(both, select_ref, 1)
    for copy in copies[2:]:
        copy.wait()
    named = neighbours_ref[...]
    ghost = jnp.maximum(named - points, 0)
    sender = ghost // capacity
    place = place_of(sender, me, parts)
    named = jnp.where(named < points, named, points + place * capacity + (ghost - sender * capacity))
    half = 0.5 * weights_ref[...]
    diagonal_ref[...] = jnp.sum(half, axis=0, keepdims=True) + potential_ref[...]
    targets = [named[k : k + 1] for k in range(count)]
    values = [half[k : k + 1] for k in range(count)]
    for k in range(count):
        for later in range(k + 1, count):
            same = targets[k] == targets[later]
            values[k] = jnp.where(same, values[k] + values[later], values[k])
            targets[later] = jnp.where(same, -1, targets[later])
    for k in range(count):
        targets_ref[k : k + 1] = targets[k]
        values_ref[k : k + 1] = values[k]
    stencil_rows(targets, values, [(near_high, near_low)], 0)


def ghost_kernel(first, targets_ref, values_ref, *outs):
    count = targets_ref.shape[0]
    targets = [targets_ref[k : k + 1] for k in range(count)]
    values = [values_ref[k : k + 1] for k in range(count)]
    stencil_rows(targets, values, list(zip(outs[::2], outs[1::2], strict=True)), first)


def intersect(both, turned):
    rows = both.shape[0] // 2
    half = rows // 2
    columns = turned.shape[1] // 4
    result = dot(both, turned)
    result = result[:rows, : 2 * columns] + result[rows:, : 2 * columns] + result[:rows, 2 * columns :]
    if columns >= LANES:
        return result[:half, :columns] + result[half:, columns:]
    result = result[:half] + pltpu.roll(result[half:], columns, 1)
    lane = lax.broadcasted_iota(jnp.int32, (half // 2, LANES), 1)
    return jnp.where(lane < columns, result[: half // 2], pltpu.roll(result[half // 2 :], columns, 1))


def exchange_term(sums, wide):
    columns = wide.shape[0] // 4
    if columns >= LANES:
        zero = jnp.zeros_like(sums)
        left = jnp.concatenate([jnp.concatenate([sums, zero], axis=1), jnp.concatenate([zero, sums], axis=1)], axis=0)
    else:
        lower = lax.broadcasted_iota(jnp.int32, sums.shape, 1) < columns
        rolled = pltpu.roll(sums, columns, 1)
        left = jnp.concatenate(
            [
                jnp.where(lower, sums, 0.0),
                jnp.where(lower, rolled, 0.0),
                jnp.where(lower, 0.0, rolled),
                jnp.where(lower, 0.0, sums),
            ],
            axis=0,
        )
    rows = left.shape[0]
    high, low = split(left)
    upper = jnp.concatenate([high, high], axis=1)
    lower = jnp.concatenate([low, jnp.zeros_like(low)], axis=1)
    result = dot(jnp.concatenate([upper, lower], axis=0), wide)
    return result[:rows] + result[rows:]


def slots_of(rows, tall, refs):
    slots = [(ref, 0) for ref in refs[: EARLY - 1]]
    if refs[0].shape[0] > rows + tall:
        return slots + [(ref, rows + tall) for ref in refs[: EARLY - 1]]
    return slots + [(refs[-1].at[at], tall) for at in range(refs[-1].shape[0])]


def packed(both, select_ref, place):
    rows = both.shape[0] // 2
    result = dot(both, select_ref[:, pl.ds(place * TILE, TILE)])
    return result[:rows] + result[rows:]


def pack(both, select_ref, tall, refs):
    rows = both.shape[0] // 2
    for place, (ref, start) in enumerate(slots_of(rows, tall, refs)):
        ref[start : start + rows, :] = packed(both, select_ref, place + 2)


def widened(partial, capacity):
    tall, width = partial.shape
    if width == capacity:
        return partial
    return jnp.concatenate([partial, jnp.zeros((tall, capacity - width), F32)], axis=1)


def spread(partial, rows, refs):
    tall = partial.shape[0]
    partial = widened(partial, refs[0].shape[1])
    for ref in refs[: EARLY - 1]:
        ref[rows : rows + tall, :] = partial
    for late_ref in refs[EARLY - 1 :]:
        for at in range(late_ref.shape[0]):
            late_ref[at, :tall, :] = partial


def start_kernel(groups, *refs):
    pieces, (field_ref, *refs) = refs[:groups], refs[groups:]
    sent = (len(refs) - 3) // 2
    (*ready, message_in), (wide_ref, turned_ref, partial_ref, *out, message_ref) = refs[:sent], refs[sent:]
    rows = field_ref.shape[0]
    pieces = [piece[...] for piece in pieces]
    if pieces[0].ndim == 4:
        pieces = [pieces[0][band] for band in range(pieces[0].shape[0])]
    real = jnp.concatenate([piece[0] for piece in pieces], axis=0)
    imag = jnp.concatenate([piece[1] for piece in pieces], axis=0)
    wide = jnp.concatenate([real, -imag, imag, real], axis=0)
    wide_ref[...] = jnp.concatenate(split(wide), axis=0)
    turned_ref[...] = jnp.concatenate(split(wide.T), axis=1)
    both, _ = stacked(field_ref[...])
    partial = intersect(both, turned_ref[...])
    partial_ref[...] = partial
    tall = partial.shape[0]
    for (source, start), (target, _) in zip(slots_of(rows, tall, ready), slots_of(rows, tall, out), strict=True):
        target[start : start + rows, :] = source[start : start + rows, :]
    spread(partial, rows, out)
    message_ref[:rows, :] = message_in[:rows, :]
    message_ref[rows:, :] = widened(partial, message_ref.shape[1])


def near_values(both, high, select_ref, near_high, near_low):
    own_both, own_high = stacked(packed(both, select_ref, 0))
    both = jnp.concatenate([both, own_both], axis=1)
    return product(both, jnp.concatenate([high, own_high], axis=1), near_high[...], near_low[...])


def near_kernel(term_ref, partial_ref, select_ref, near_high, near_low, diagonal_ref, base_ref, message_ref):
    rows = term_ref.shape[0]
    term = term_ref[...]
    both, high = stacked(term)
    message_ref[:rows, :] = packed(both, select_ref, 1)
    message_ref[rows:, :] = widened(partial_ref[...], message_ref.shape[1])
    base_ref[...] = term * diagonal_ref[...] - near_values(both, high, select_ref, near_high, near_low)


def first_near_kernel(first, term_ref, select_ref, near_high, near_low, diagonal_ref, targets_ref, values_ref, base_ref, *outs):
    ghost_kernel(first, targets_ref, values_ref, *outs)
    term = term_ref[...]
    both, high = stacked(term)
    base_ref[...] = term * diagonal_ref[...] - near_values(both, high, select_ref, near_high, near_low)


def ghost_values(blocks, high, low):
    pieces = [stacked(block) for block in blocks]
    both = jnp.concatenate([piece[0] for piece in pieces], axis=1)
    return product(both, jnp.concatenate([piece[1] for piece in pieces], axis=1), high, low)


def early_kernel(base_ref, partial_ref, early_high, early_low, *refs):
    early_refs, (base_out, sums_out) = refs[:-2], refs[-2:]
    rows = base_ref.shape[0]
    sums = partial_ref[...]
    tall, width = sums.shape
    for ref in early_refs:
        sums = sums + ref[rows : rows + tall, :width]
    sums_out[...] = sums
    base_out[...] = base_ref[...] - ghost_values([ref[:rows, :] for ref in early_refs], early_high[...], early_low[...])


def late_kernel(order, last, late_ref, base_ref, sums_ref, total_ref, select_ref, first_high, first_low, rest_high, rest_low, wide_ref, turned_ref, *outs):
    half = base_ref.shape[0] // 2
    blocks = range(late_ref.shape[0])
    sums = sums_ref[...]
    tall, width = sums.shape
    for block in blocks:
        sums = sums + late_ref[block, :tall, :width]
    ghosts = [late_ref[block, tall:, :] for block in blocks]
    cut = first_high.shape[0] // late_ref.shape[2]
    image = base_ref[...] - exchange_term(sums, wide_ref[...])
    image = image - ghost_values(ghosts[:cut], first_high[...], first_low[...])
    image = image - ghost_values(ghosts[cut:], rest_high[...], rest_low[...])
    scale = time_step / order
    term = jnp.concatenate([scale * image[half:], -scale * image[:half]], axis=0)
    outs[0][...] = total_ref[...] + term
    if last:
        return
    _, term_ref, partial_ref, *out = outs
    term_ref[...] = term
    both, _ = stacked(term)
    partial = intersect(both, turned_ref[...])
    partial_ref[...] = partial
    pack(both, select_ref, tall, out)
    spread(partial, term.shape[0], out)


def swap(value, bits, parts):
    return lax.ppermute(value, "mesh", [(part, part ^ bits) for part in range(parts)])


def move(value, offset, parts):
    return lax.ppermute(value, "mesh", [(part, (part + offset) % parts) for part in range(parts)])


def gather_frozen(frozen):
    bands = lax.axis_size("band")
    if bands == 4:
        return [lax.ppermute(frozen, "band", [(at, at ^ step) for at in range(bands)]) for step in (2, 1, 3)]
    return [lax.all_gather(frozen, "band", axis=0, tiled=False)]


def body(states, frozen, weights, potential, send_list, neighbours):
    parts = lax.axis_size("mesh")
    points = states.shape[2]
    rows = 2 * states.shape[1]
    half = rows // 2
    capacity = send_list.shape[2]
    relations = blocks_of(parts)
    places = len(relations)
    paired = parts == 8
    me = lax.axis_index("mesh").astype(jnp.int32).reshape(1)
    count = neighbours.shape[0]

    bands = lax.axis_size("band")
    pieces = gather_frozen(frozen)
    columns = 2 * bands * frozen.shape[1]
    sum_shape = (half, columns) if columns >= LANES else (half * columns // LANES, LANES)
    tall = rows + sum_shape[0]
    late_blocks = places - 1 - EARLY
    outgoing = [((tall + rows if paired else tall, capacity), F32)] * (EARLY - 1)
    if not paired:
        outgoing += [((late_blocks, tall, capacity), F32)]
    near_rows, early_rows = points + capacity, EARLY * capacity
    first_rows = LATE_FIRST * capacity
    rest_rows = late_blocks * capacity - first_rows
    targets, values, diagonal, select, near_high, near_low, field, own_frozen, *sent = call(
        functools.partial(plan_kernel, parts, sum_shape[0]),
        [((count, points), jnp.int32), ((count, points), F32), ((1, points), F32), ((points, places * capacity), BF16)]
        + [((near_rows, points), BF16)] * 2
        + [((rows, points), F32), (frozen.shape, F32)]
        + outgoing
        + [((tall, capacity), F32)],
        (6 * near_rows * points, 12 << 20),
        me, send_list, states.reshape(rows, points), neighbours, weights, potential.reshape(1, points), frozen,
        scalars=1,
        remote=6,
        scratch=[
            pltpu.VMEM(send_list.shape, jnp.int32),
            pltpu.VMEM(neighbours.shape, jnp.int32),
            pltpu.VMEM(weights.shape, F32),
            pltpu.VMEM((1, points), F32),
            pltpu.SemaphoreType.DMA((6,)),
        ],
    )
    if len(pieces) == bands - 1:
        pieces = [own_frozen, *pieces]
    wide, turned, partial, *sent, message = call(
        functools.partial(start_kernel, len(pieces)),
        [((4 * columns, points), BF16), ((points, 4 * columns), BF16), (sum_shape, F32)] + outgoing + [((tall, capacity), F32)],
        (6 * rows * points * 2 * columns, 4 << 20),
        *pieces, field, *sent,
    )
    sent[0], field, diagonal, targets = lax.optimization_barrier((sent[0], field, diagonal, targets))
    total, term = field, field
    for order in range(1, TERMS + 1):
        if paired:
            early = [swap(block, bits, parts) for block, bits in zip(sent, relations[2:], strict=False)]
        else:
            early = [move(block, offset, parts) for block, offset in zip(sent[: EARLY - 1], relations[2:], strict=False)]
        if order == 1:
            base, early_high, early_low, first_high, first_low = call(
                functools.partial(first_near_kernel, near_rows),
                [((rows, points), F32)] + [((early_rows, points), BF16)] * 2 + [((first_rows, points), BF16)] * 2,
                (6 * rows * points * near_rows, 16 << 20),
                term, select, near_high, near_low, diagonal, targets, values,
            )
        else:
            base, message = call(
                near_kernel,
                [((rows, points), F32), ((tall, capacity), F32)],
                (6 * rows * points * near_rows, 16 << 20),
                term, partial, select, near_high, near_low, diagonal,
            )
        if paired:
            message = swap(message, 1, parts)
            late = jnp.stack([block[rows:] for block in early])
            late, message, base, near_high, near_low, diagonal, targets = lax.optimization_barrier(
                (late, message, base, near_high, near_low, diagonal, targets)
            )
            late = swap(late, 1, parts)
        else:
            message = move(message, relations[1], parts)
            late = jnp.stack([move(sent[-1][at], offset, parts) for at, offset in enumerate(relations[1 + EARLY :])])
        if order == 1:
            rest_high, rest_low = call(
                functools.partial(ghost_kernel, near_rows + early_rows + first_rows),
                [((rest_rows, points), BF16)] * 2,
                (6 * rest_rows * points, 12 << 20),
                targets, values,
            )
        base, sums = call(
            early_kernel,
            [((rows, points), F32), (sum_shape, F32)],
            (6 * rows * points * early_rows, 4 << 20),
            base, partial, early_high, early_low, message, *early,
        )
        last = order == TERMS
        shapes = [((rows, points), F32)]
        if not last:
            shapes += [((rows, points), F32), (sum_shape, F32)] + outgoing
        outs = call(
            functools.partial(late_kernel, order, last),
            shapes,
            (6 * rows * points * (first_rows + rest_rows), 12 << 20),
            late, base, sums, total, select, first_high, first_low, rest_high, rest_low,
            wide, turned,
        )
        total = outs[0]
        if not last:
            _, term, partial, *sent = outs
    return total.reshape(states.shape)


def solution(mesh):
    return jax.shard_map(
        body,
        mesh=mesh,
        in_specs=(
            P(None, "band", "mesh"),
            P(None, "band", "mesh"),
            P(None, "mesh"),
            P("mesh"),
            P("mesh", None, None),
            P(None, "mesh"),
        ),
        out_specs=P(None, "band", "mesh"),
        check_vma=False,
    )
```

```python
import functools

import jax
import jax.numpy as jnp
from jax import lax
from jax.experimental import pallas as pl
from jax.experimental.pallas import tpu as pltpu
from jax.sharding import PartitionSpec as P

TERMS = 4
REACH = 3
LANES = 128
TILE = 256

time_step = 0.3

F32, BF16 = jnp.float32, jnp.bfloat16
VMEM_LIMIT = 24 << 20


def split(value):
    high = value.astype(BF16)
    return high, (value - high.astype(F32)).astype(BF16)


def stacked(value):
    high, low = split(value)
    return jnp.concatenate([high, low], axis=0), high


def dot(left, right):
    return lax.dot_general(left, right, (((1,), (0,)), ((), ())), preferred_element_type=F32)


def product(both, high, right_high, right_low):
    rows = high.shape[0]
    result = dot(both, right_high)
    return result[:rows] + result[rows:] + dot(high, right_low)


def blocks_of(parts):
    if parts == 8:
        return [0, 1, 6, 4, 2, 7, 5, 3]
    relative = [0]
    for offset in [*range(1, REACH + 1), *range(-REACH, 0), parts // 2]:
        if offset % parts not in relative:
            relative.append(offset % parts)
    return relative


EARLY = 4
LATE_FIRST = 1


def receiver_of(me, block, parts):
    return me ^ block if parts == 8 else lax.rem(me + block, parts)


def place_of(sender, me, parts):
    relative = sender ^ me if parts == 8 else lax.rem(me - sender + parts, parts)
    result = jnp.zeros_like(relative)
    for place, block in enumerate(blocks_of(parts)):
        result = jnp.where(relative == block, place, result)
    return result


def call(kernel, out_shape, cost, *args, scalars=0, remote=0, scratch=()):
    held = slice(scalars, scalars + remote)
    args = list(args)
    args[held] = [pltpu.with_memory_space_constraint(arg, pltpu.HBM) for arg in args[held]]
    spaces = [pltpu.SMEM] * scalars + [pltpu.HBM] * remote + [pltpu.VMEM] * (len(args) - scalars - remote)
    return pl.pallas_call(
        kernel,
        out_shape=[jax.ShapeDtypeStruct(shape, dtype) for shape, dtype in out_shape],
        in_specs=[pl.BlockSpec(memory_space=space) for space in spaces],
        out_specs=[pl.BlockSpec(memory_space=pltpu.VMEM)] * len(out_shape),
        scratch_shapes=scratch,
        compiler_params=pltpu.CompilerParams(vmem_limit_bytes=VMEM_LIMIT),
        cost_estimate=pl.CostEstimate(flops=cost[0], bytes_accessed=cost[1], transcendentals=0),
    )(*args)


def stencil_rows(targets, values, outs, first):
    tall, chunk = 16, 2 * LANES
    points = targets[0].shape[1]
    row_id = lax.broadcasted_iota(jnp.int32, (tall, chunk), 0).astype(jnp.int16)
    zero = jnp.zeros((tall, chunk), BF16)
    for lane in range(0, points, chunk):
        at = [jnp.broadcast_to(t[:, lane : lane + chunk], (tall, chunk)).astype(jnp.int16) for t in targets]
        pieces = [split(jnp.broadcast_to(v[:, lane : lane + chunk], (tall, chunk))) for v in values]
        base = first
        for high_ref, low_ref in outs:

            @pl.loop(0, high_ref.shape[0] // TILE)
            def _(tile, base=base, high_ref=high_ref, low_ref=low_ref):
                start = (base + tile * TILE).astype(jnp.int16)
                local = [a - start for a in at]
                for row in range(0, TILE, tall):
                    here = row_id + jnp.int16(row)
                    high, low = zero, zero
                    for target, (value_high, value_low) in zip(local, pieces, strict=True):
                        hit = target == here
                        high = jnp.where(hit, value_high, high)
                        low = jnp.where(hit, value_low, low)
                    place = pl.multiple_of(tile * TILE + row, tall)
                    high_ref[pl.ds(place, tall), lane : lane + chunk] = high
                    low_ref[pl.ds(place, tall), lane : lane + chunk] = low

            base = base + high_ref.shape[0]


def plan_kernel(parts, tall, me_ref, *refs):
    sources, refs = refs[:6], refs[6:]
    targets_ref, values_ref, diagonal_ref, select_ref, near_high, near_low, field_ref, frozen_ref, *refs = refs
    out, (routes_ref, neighbours_ref, weights_ref, potential_ref, arrival) = refs[:-5], refs[-5:]
    arrays = [routes_ref, field_ref, neighbours_ref, weights_ref, potential_ref, frozen_ref]
    copies = [
        pltpu.make_async_copy(source, array, arrival.at[at])
        for at, (source, array) in enumerate(zip(sources, arrays, strict=True))
    ]
    for copy in copies:
        copy.start()
    count, points = neighbours_ref.shape
    capacity = routes_ref.shape[2]
    rows = field_ref.shape[0]
    me = me_ref[0]
    copies[0].wait()
    copies[1].wait()
    step = 16
    row_id = lax.broadcasted_iota(jnp.int32, (step, capacity), 0).astype(jnp.int16)
    one, zero = jnp.ones((step, capacity), BF16), jnp.zeros((step, capacity), BF16)
    for place, block in enumerate(blocks_of(parts)):
        route = routes_ref[0, pl.ds(receiver_of(me, block, parts), 1), :]
        route = jnp.broadcast_to(route, (step, capacity)).astype(jnp.int16)
        for row in range(0, points, step):
            hit = route == row_id + jnp.int16(row)
            select_ref[row : row + step, pl.ds(place * capacity, capacity)] = jnp.where(hit, one, zero)
    both, _ = stacked(field_ref[...])
    *out, message_ref = out
    pack(both, select_ref, tall, out)
    message_ref[: field_ref.shape[0], :] = packed(both, select_ref, 1)
    for copy in copies[2:]:
        copy.wait()
    named = neighbours_ref[...]
    ghost = jnp.maximum(named - points, 0)
    sender = ghost // capacity
    place = place_of(sender, me, parts)
    named = jnp.where(named < points, named, points + place * capacity + (ghost - sender * capacity))
    half = 0.5 * weights_ref[...]
    diagonal_ref[...] = jnp.sum(half, axis=0, keepdims=True) + potential_ref[...]
    targets = [named[k : k + 1] for k in range(count)]
    values = [half[k : k + 1] for k in range(count)]
    for k in range(count):
        for later in range(k + 1, count):
            same = targets[k] == targets[later]
            values[k] = jnp.where(same, values[k] + values[later], values[k])
            targets[later] = jnp.where(same, -1, targets[later])
    for k in range(count):
        targets_ref[k : k + 1] = targets[k]
        values_ref[k : k + 1] = values[k]
    stencil_rows(targets, values, [(near_high, near_low)], 0)


def ghost_kernel(first, targets_ref, values_ref, *outs):
    count = targets_ref.shape[0]
    targets = [targets_ref[k : k + 1] for k in range(count)]
    values = [values_ref[k : k + 1] for k in range(count)]
    stencil_rows(targets, values, list(zip(outs[::2], outs[1::2], strict=True)), first)


def intersect(both, turned):
    rows = both.shape[0] // 2
    half = rows // 2
    columns = turned.shape[1] // 4
    result = dot(both, turned)
    result = result[:rows, : 2 * columns] + result[rows:, : 2 * columns] + result[:rows, 2 * columns :]
    if columns >= LANES:
        return result[:half, :columns] + result[half:, columns:]
    result = result[:half] + pltpu.roll(result[half:], columns, 1)
    lane = lax.broadcasted_iota(jnp.int32, (half // 2, LANES), 1)
    return jnp.where(lane < columns, result[: half // 2], pltpu.roll(result[half // 2 :], columns, 1))


def exchange_term(sums, wide):
    columns = wide.shape[0] // 4
    if columns >= LANES:
        zero = jnp.zeros_like(sums)
        left = jnp.concatenate([jnp.concatenate([sums, zero], axis=1), jnp.concatenate([zero, sums], axis=1)], axis=0)
    else:
        lower = lax.broadcasted_iota(jnp.int32, sums.shape, 1) < columns
        rolled = pltpu.roll(sums, columns, 1)
        left = jnp.concatenate(
            [
                jnp.where(lower, sums, 0.0),
                jnp.where(lower, rolled, 0.0),
                jnp.where(lower, 0.0, rolled),
                jnp.where(lower, 0.0, sums),
            ],
            axis=0,
        )
    rows = left.shape[0]
    high, low = split(left)
    upper = jnp.concatenate([high, high], axis=1)
    lower = jnp.concatenate([low, jnp.zeros_like(low)], axis=1)
    result = dot(jnp.concatenate([upper, lower], axis=0), wide)
    return result[:rows] + result[rows:]


def slots_of(rows, tall, refs):
    slots = [(ref, 0) for ref in refs[: EARLY - 1]]
    if refs[0].shape[0] > rows + tall:
        return slots + [(ref, rows + tall) for ref in refs[: EARLY - 1]]
    return slots + [(refs[-1].at[at], tall) for at in range(refs[-1].shape[0])]


def packed(both, select_ref, place):
    rows = both.shape[0] // 2
    result = dot(both, select_ref[:, pl.ds(place * TILE, TILE)])
    return result[:rows] + result[rows:]


def pack(both, select_ref, tall, refs):
    rows = both.shape[0] // 2
    for place, (ref, start) in enumerate(slots_of(rows, tall, refs)):
        ref[start : start + rows, :] = packed(both, select_ref, place + 2)


def widened(partial, capacity):
    tall, width = partial.shape
    if width == capacity:
        return partial
    return jnp.concatenate([partial, jnp.zeros((tall, capacity - width), F32)], axis=1)


def spread(partial, rows, refs):
    tall = partial.shape[0]
    partial = widened(partial, refs[0].shape[1])
    for ref in refs[: EARLY - 1]:
        ref[rows : rows + tall, :] = partial
    for late_ref in refs[EARLY - 1 :]:
        for at in range(late_ref.shape[0]):
            late_ref[at, :tall, :] = partial


def start_kernel(groups, *refs):
    pieces, (field_ref, *refs) = refs[:groups], refs[groups:]
    sent = (len(refs) - 3) // 2
    (*ready, message_in), (wide_ref, turned_ref, partial_ref, *out, message_ref) = refs[:sent], refs[sent:]
    rows = field_ref.shape[0]
    pieces = [piece[...] for piece in pieces]
    if pieces[0].ndim == 4:
        pieces = [pieces[0][band] for band in range(pieces[0].shape[0])]
    real = jnp.concatenate([piece[0] for piece in pieces], axis=0)
    imag = jnp.concatenate([piece[1] for piece in pieces], axis=0)
    wide = jnp.concatenate([real, -imag, imag, real], axis=0)
    wide_ref[...] = jnp.concatenate(split(wide), axis=0)
    turned_ref[...] = jnp.concatenate(split(wide.T), axis=1)
    both, _ = stacked(field_ref[...])
    partial = intersect(both, turned_ref[...])
    partial_ref[...] = partial
    tall = partial.shape[0]
    for (source, start), (target, _) in zip(slots_of(rows, tall, ready), slots_of(rows, tall, out), strict=True):
        target[start : start + rows, :] = source[start : start + rows, :]
    spread(partial, rows, out)
    message_ref[:rows, :] = message_in[:rows, :]
    message_ref[rows:, :] = widened(partial, message_ref.shape[1])


def near_values(both, high, select_ref, near_high, near_low):
    own_both, own_high = stacked(packed(both, select_ref, 0))
    both = jnp.concatenate([both, own_both], axis=1)
    return product(both, jnp.concatenate([high, own_high], axis=1), near_high[...], near_low[...])


def near_kernel(term_ref, total_ref, partial_ref, select_ref, near_high, near_low, diagonal_ref, base_ref, message_ref, total_out):
    rows = term_ref.shape[0]
    term = term_ref[...]
    total_out[...] = total_ref[...] + term
    both, high = stacked(term)
    message_ref[:rows, :] = packed(both, select_ref, 1)
    message_ref[rows:, :] = widened(partial_ref[...], message_ref.shape[1])
    base_ref[...] = term * diagonal_ref[...] - near_values(both, high, select_ref, near_high, near_low)


def first_near_kernel(first, term_ref, select_ref, near_high, near_low, diagonal_ref, targets_ref, values_ref, base_ref, *outs):
    ghost_kernel(first, targets_ref, values_ref, *outs)
    term = term_ref[...]
    both, high = stacked(term)
    base_ref[...] = term * diagonal_ref[...] - near_values(both, high, select_ref, near_high, near_low)


def ghost_values(blocks, high, low):
    pieces = [stacked(block) for block in blocks]
    both = jnp.concatenate([piece[0] for piece in pieces], axis=1)
    return product(both, jnp.concatenate([piece[1] for piece in pieces], axis=1), high, low)


def early_kernel(base_ref, partial_ref, early_high, early_low, *refs):
    early_refs, (base_out, sums_out) = refs[:-2], refs[-2:]
    rows = base_ref.shape[0]
    sums = partial_ref[...]
    tall, width = sums.shape
    for ref in early_refs:
        sums = sums + ref[rows : rows + tall, :width]
    sums_out[...] = sums
    base_out[...] = base_ref[...] - ghost_values([ref[:rows, :] for ref in early_refs], early_high[...], early_low[...])


def late_kernel(order, last, late_ref, base_ref, sums_ref, total_ref, select_ref, first_high, first_low, rest_high, rest_low, wide_ref, turned_ref, *outs):
    half = base_ref.shape[0] // 2
    blocks = range(late_ref.shape[0])
    sums = sums_ref[...]
    tall, width = sums.shape
    for block in blocks:
        sums = sums + late_ref[block, :tall, :width]
    ghosts = [late_ref[block, tall:, :] for block in blocks]
    cut = first_high.shape[0] // late_ref.shape[2]
    image = base_ref[...] - exchange_term(sums, wide_ref[...])
    image = image - ghost_values(ghosts[:cut], first_high[...], first_low[...])
    image = image - ghost_values(ghosts[cut:], rest_high[...], rest_low[...])
    scale = time_step / order
    term = jnp.concatenate([scale * image[half:], -scale * image[:half]], axis=0)
    if last:
        outs[0][...] = total_ref[...] + term
        return
    term_ref, partial_ref, *out = outs
    term_ref[...] = term
    both, _ = stacked(term)
    partial = intersect(both, turned_ref[...])
    partial_ref[...] = partial
    pack(both, select_ref, tall, out)
    spread(partial, term.shape[0], out)


def swap(value, bits, parts):
    return lax.ppermute(value, "mesh", [(part, part ^ bits) for part in range(parts)])


def move(value, offset, parts):
    return lax.ppermute(value, "mesh", [(part, (part + offset) % parts) for part in range(parts)])


def gather_frozen(frozen):
    bands = lax.axis_size("band")
    if bands == 4:
        return [lax.ppermute(frozen, "band", [(at, at ^ step) for at in range(bands)]) for step in (2, 1, 3)]
    return [lax.all_gather(frozen, "band", axis=0, tiled=False)]


def body(states, frozen, weights, potential, send_list, neighbours):
    parts = lax.axis_size("mesh")
    points = states.shape[2]
    rows = 2 * states.shape[1]
    half = rows // 2
    capacity = send_list.shape[2]
    relations = blocks_of(parts)
    places = len(relations)
    paired = parts == 8
    me = lax.axis_index("mesh").astype(jnp.int32).reshape(1)
    count = neighbours.shape[0]

    bands = lax.axis_size("band")
    pieces = gather_frozen(frozen)
    columns = 2 * bands * frozen.shape[1]
    sum_shape = (half, columns) if columns >= LANES else (half * columns // LANES, LANES)
    tall = rows + sum_shape[0]
    late_blocks = places - 1 - EARLY
    outgoing = [((tall + rows if paired else tall, capacity), F32)] * (EARLY - 1)
    if not paired:
        outgoing += [((late_blocks, tall, capacity), F32)]
    near_rows, early_rows = points + capacity, EARLY * capacity
    first_rows = LATE_FIRST * capacity
    rest_rows = late_blocks * capacity - first_rows
    targets, values, diagonal, select, near_high, near_low, field, own_frozen, *sent = call(
        functools.partial(plan_kernel, parts, sum_shape[0]),
        [((count, points), jnp.int32), ((count, points), F32), ((1, points), F32), ((points, places * capacity), BF16)]
        + [((near_rows, points), BF16)] * 2
        + [((rows, points), F32), (frozen.shape, F32)]
        + outgoing
        + [((tall, capacity), F32)],
        (6 * near_rows * points, 12 << 20),
        me, send_list, states.reshape(rows, points), neighbours, weights, potential.reshape(1, points), frozen,
        scalars=1,
        remote=6,
        scratch=[
            pltpu.VMEM(send_list.shape, jnp.int32),
            pltpu.VMEM(neighbours.shape, jnp.int32),
            pltpu.VMEM(weights.shape, F32),
            pltpu.VMEM((1, points), F32),
            pltpu.SemaphoreType.DMA((6,)),
        ],
    )
    if len(pieces) == bands - 1:
        pieces = [own_frozen, *pieces]
    wide, turned, partial, *sent, message = call(
        functools.partial(start_kernel, len(pieces)),
        [((4 * columns, points), BF16), ((points, 4 * columns), BF16), (sum_shape, F32)] + outgoing + [((tall, capacity), F32)],
        (6 * rows * points * 2 * columns, 4 << 20),
        *pieces, field, *sent,
    )
    sent[0], field, diagonal, targets = lax.optimization_barrier((sent[0], field, diagonal, targets))
    total, term = field, field
    for order in range(1, TERMS + 1):
        if paired:
            early = [swap(block, bits, parts) for block, bits in zip(sent, relations[2:], strict=False)]
        else:
            early = [move(block, offset, parts) for block, offset in zip(sent[: EARLY - 1], relations[2:], strict=False)]
        before = total
        if order == 1:
            base, early_high, early_low, first_high, first_low = call(
                functools.partial(first_near_kernel, near_rows),
                [((rows, points), F32)] + [((early_rows, points), BF16)] * 2 + [((first_rows, points), BF16)] * 2,
                (6 * rows * points * near_rows, 16 << 20),
                term, select, near_high, near_low, diagonal, targets, values,
            )
        else:
            base, message, total = call(
                near_kernel,
                [((rows, points), F32), ((tall, capacity), F32), ((rows, points), F32)],
                (6 * rows * points * near_rows, 16 << 20),
                term, total, partial, select, near_high, near_low, diagonal,
            )
        if paired:
            message = swap(message, 1, parts)
            late = jnp.stack([block[rows:] for block in early])
            late, message, base, near_high, near_low, diagonal, targets, _, _ = lax.optimization_barrier(
                (late, message, base, near_high, near_low, diagonal, targets, before, term)
            )
            late = swap(late, 1, parts)
        else:
            message = move(message, relations[1], parts)
            late = jnp.stack([move(sent[-1][at], offset, parts) for at, offset in enumerate(relations[1 + EARLY :])])
        if order == 1:
            rest_high, rest_low = call(
                functools.partial(ghost_kernel, near_rows + early_rows + first_rows),
                [((rest_rows, points), BF16)] * 2,
                (6 * rest_rows * points, 12 << 20),
                targets, values,
            )
        base, sums = call(
            early_kernel,
            [((rows, points), F32), (sum_shape, F32)],
            (6 * rows * points * early_rows, 4 << 20),
            base, partial, early_high, early_low, message, *early,
        )
        last = order == TERMS
        shapes = [((rows, points), F32)]
        if not last:
            shapes += [(sum_shape, F32)] + outgoing
        outs = call(
            functools.partial(late_kernel, order, last),
            shapes,
            (6 * rows * points * (first_rows + rest_rows), 12 << 20),
            late, base, sums, total, select, first_high, first_low, rest_high, rest_low,
            wide, turned,
        )
        if not last:
            term, partial, *sent = outs
    return outs[0].reshape(states.shape)


def solution(mesh):
    return jax.shard_map(
        body,
        mesh=mesh,
        in_specs=(
            P(None, "band", "mesh"),
            P(None, "band", "mesh"),
            P(None, "mesh"),
            P("mesh"),
            P("mesh", None, None),
            P(None, "mesh"),
        ),
        out_specs=P(None, "band", "mesh"),
        check_vma=False,
    )
```
